512 devices in a mesh: row: 16 (over z_hi, y, core), col: 32 (over x, z_lo).
Axes of the slice: x: 4, y: 4, z: 16 (z_hi: 2, z_lo: 8; z = z_hi * 8 + z_lo), core: 2. Of those that a mesh axis runs over, the one named last changes fastest.
Arguments:
- left_blocks: bfloat16 [16, 32, 2, 8, 64, 64], P('row', 'col'), may hold values from -0.375 to 0.375
- left_cols: int32 [16, 32, 2, 8], P('row', 'col'), may hold values from 0 to 15, all different within a row
- right_blocks: bfloat16 [16, 32, 16, 6, 64, 64], P('row', 'col'), may hold values from -6 to 6
- right_cols: int32 [16, 32, 16, 6], P('row', 'col'), may hold values from 0 to 15, all different within a row
- out_cols: int32 [16, 32, 2, 8], P('row', 'col'), may hold values from 0 to 15, all different within a row
Outputs:
- product: float32 [16, 32, 2, 8, 64, 64], P('row', 'col')
The draws below stay inside these ranges and needn't reach their ends.
Inputs may be any that keep to these rules, and one draw needn't show every extreme that they name: `left_cols`: the entries of one block row are distinct. `right_cols`: the entries of one block row are distinct. `out_cols`: the entries of one block row are distinct.
All inputs are finite; a program needn't handle non-finite values.
Results may differ from the reference program's by a relative error of at most 0.0003.
Values may be sent and summed in bfloat16 or wider, within the bound.
A program may use at most 64 MiB of HBM per device.

```python
import jax
import jax.numpy as jnp
from jax import lax

BS = 64
IB = 2
KB = 16
JB = 16
NL = 8
NR = 6
NO = 8
TICKS = 8
N_ROW = 16
N_COL = 32


def level_of(own_key, shape, cuts, least, high):
    gain = 1.0
    for dim, parts in cuts:
        draws = jax.random.uniform(jax.random.fold_in(jax.random.fold_in(own_key, 6), dim), (parts,), jnp.float32, least / len(cuts), high / len(cuts))
        gain = gain * jnp.repeat(jnp.exp(draws), shape[dim] // parts).reshape((-1,) + (1,) * (len(shape) - 1 - dim))
    return gain


def picks_of(rng, rows, number_of, top, lift):
    sequence = jax.random.permutation(jax.random.fold_in(rng, 1), number_of)
    boost = sequence
    for power in range(3):
        boost = boost * boost // number_of
    boost = boost * lift // number_of
    chance = jax.random.randint(jax.random.fold_in(rng, 2), (rows, number_of), 0, 4096) + boost
    sure = jax.random.permutation(jax.random.fold_in(rng, 3), rows)[jnp.arange(number_of) % rows]
    chance = jnp.where(jnp.arange(rows)[:, None] == sure[None, :], 1 << 14, chance)
    score = chance * number_of + jnp.arange(number_of)
    return lax.top_k(score.astype(jnp.int32), top)[1].astype(jnp.int32)


def bell_draw(key, shape, spread, limit, pieces=(), kind=jnp.bfloat16):
    entries = spread * jax.random.normal(key, shape, jnp.float32)
    if pieces:
        entries = entries * level_of(key, shape, pieces, -0.22, 0.18)
    return jnp.clip(entries, -limit, limit).astype(kind)


def setup_inputs(seed: int = 0) -> dict:
    key_list = jax.random.split(jax.random.key(seed), 6)
    return {
        "left_blocks": bell_draw(key_list[0], (N_ROW, N_COL, IB, NL, BS, BS), (BS * 4) ** -0.5, 0.375, ((0, 16), (1, 32))),
        "left_cols": picks_of(key_list[1], N_ROW * N_COL * IB, KB, NL, 0).reshape((N_ROW, N_COL, IB, NL)),
        "right_blocks": bell_draw(key_list[2], (N_ROW, N_COL, KB, NR, BS, BS), 1.0, 6.0, ((0, 16), (1, 32))),
        "right_cols": picks_of(key_list[3], N_ROW * N_COL * KB, JB, NR, 0).reshape((N_ROW, N_COL, KB, NR)),
        "out_cols": picks_of(key_list[4], N_ROW * N_COL * IB, JB, NO, 0).reshape((N_ROW, N_COL, IB, NO)),
    }


def one_tick(left, left_cols, right, right_cols, pattern):
    inner = right.shape[0]
    pick_row = (left_cols[:, :, None] == jnp.arange(inner, dtype=jnp.int32)[None, None, :]).astype(jnp.float32)
    match = (right_cols[None, None, :, :] == pattern[:, :, None, None]).astype(jnp.float32)
    select = jnp.einsum('iak,iokb->iaokb', pick_row, match).astype(jnp.bfloat16)
    chosen = jnp.einsum('iaokb,kbyz->iaoyz', select, right, preferred_element_type=jnp.float32).astype(jnp.bfloat16)
    return jnp.einsum('iaxy,iaoyz->ioxz', left, chosen, preferred_element_type=jnp.float32)


def reference(left_blocks, left_cols, right_blocks, right_cols, out_cols):
    def panel(flat):
        row_index = flat // N_COL
        col_index = flat % N_COL
        total = jnp.zeros((IB, NO, BS, BS), jnp.float32)
        for step in range(TICKS):
            source_row = ((row_index - step) % N_ROW).astype(jnp.int32)
            source_col = ((col_index - TICKS + 1 + step) % N_COL).astype(jnp.int32)
            total = total + one_tick(left_blocks[source_row, source_col], left_cols[source_row, source_col], right_blocks[row_index, source_col], right_cols[row_index, source_col], out_cols[row_index, col_index])
        return total
    panels = lax.map(panel, jnp.arange(N_ROW * N_COL, dtype=jnp.int32))
    return panels.reshape(N_ROW, N_COL, IB, NO, BS, BS)
```

```python
import functools

import jax
import jax.numpy as jnp
from jax import lax
from jax.experimental import pallas as pl
from jax.experimental.pallas import tpu as pltpu
from jax.sharding import PartitionSpec as P

TICKS = 8
NEAR = TICKS - 1
MESH = pl.DeviceIdType.MESH


def kernel(
    n_row, n_col, left_hbm, left_cols, right_hbm, right_cols, out_cols, out_ref,
    lraw, rraw, lbuf, dense, wide, part, acc, lcol, ocol,
    local_sem, lc_send, lc_recv, oc_send, oc_recv, far_send, far_recv, y_send, y_recv, sib_send, sib_recv, sum_send, sum_recv,
):
    row = lax.axis_index("row")
    col = lax.axis_index("col")
    y = lax.rem(row // 2, 4)
    half = row // 8
    core = lax.rem(row, 2)
    far = lax.rem(row + 8, n_row)
    sibling = row + 1 - 2 * core
    ib, nl, bs, _ = lraw.shape
    kb = rraw.shape[0]
    nr = rraw.shape[1] - 1
    no = ocol.shape[2]

    get_left = pltpu.make_async_copy(left_hbm, lraw, local_sem.at[0])
    get_right = pltpu.make_async_copy(right_hbm, rraw.at[:, pl.ds(0, nr)], local_sem.at[1])
    get_left.start()
    get_right.start()

    barrier = pltpu.get_barrier_semaphore()
    for d in range(1, n_row):
        pl.semaphore_signal(barrier, inc=1, device_id={"row": lax.rem(row + d, n_row)}, device_id_type=MESH)
    for d in range(1, TICKS):
        for e in (d, n_col - d):
            pl.semaphore_signal(barrier, inc=1, device_id={"col": lax.rem(col + e, n_col)}, device_id_type=MESH)

    def remote(src, dst, send, recv, to):
        return pltpu.make_async_remote_copy(
            src_ref=src, dst_ref=dst, send_sem=send, recv_sem=recv, device_id=to, device_id_type=MESH
        )

    get_left.wait()
    for b in range(ib):
        for a in range(0, nl, 2):
            lbuf[0, b * bs : (b + 1) * bs, a * bs : (a + 2) * bs] = jnp.concatenate(
                [lraw[b, a], lraw[b, a + 1]], axis=1
            )
    for b in range(ib):
        for a in range(nl):
            lcol[0, b, a] = left_cols[b, a]
    for i in range(kb):
        rraw[i, nr] = jnp.zeros((bs, bs), rraw.dtype)

    pl.semaphore_wait(barrier, n_row - 1 + 2 * NEAR)

    def send_ocol(s):
        return remote(out_cols, ocol.at[s], oc_send.at[s], oc_recv.at[s], {"col": lax.rem(col + n_col - NEAR + s, n_col)})

    def send_lcol(s):
        return remote(left_cols, lcol.at[s], lc_send.at[s], lc_recv.at[s], {"row": lax.rem(row + s, n_row)})

    to_far = remote(lbuf.at[0], lbuf.at[TICKS], far_send, far_recv, {"row": far})

    def to_y(d, src):
        return remote(
            lbuf.at[src], lbuf.at[2 * d], y_send.at[d - 1], y_recv.at[d - 1],
            {"row": half * 8 + lax.rem(y + d, 4) * 2 + core},
        )

    def to_sibling(i, src, dst):
        return remote(lbuf.at[src], lbuf.at[dst], sib_send.at[i], sib_recv.at[i], {"row": sibling})

    send_ocol(0).start()
    to_far.start()
    for d in range(1, 4):
        @pl.when(y + d < 4)
        def _():
            to_y(d, 0).start()

    @pl.when(core == 0)
    def _():
        to_sibling(0, 0, 1).start()

    for s in range(1, TICKS):
        if s < NEAR:
            send_ocol(s).start()
        send_lcol(s).start()
    for b in range(ib):
        for o in range(no):
            ocol[NEAR, b, o] = out_cols[b, o]

    get_right.wait()

    def fill(k, carry):
        cols = [right_cols[k, e] for e in range(nr)]

        def slot_of(j):
            slot = jnp.int32(nr)
            for e in range(nr):
                slot = jnp.where(cols[e] == j, e, slot)
            return slot

        for j in range(0, 16, 2):
            dense[k, :, j * bs : (j + 2) * bs] = jnp.concatenate(
                [rraw[k, slot_of(j)], rraw[k, slot_of(j + 1)]], axis=1
            )
        return carry

    lax.fori_loop(0, kb, fill, 0)

    low = lax.broadcasted_iota(jnp.int32, (bs, 2 * bs), 1) < bs

    def product(s):
        for b in range(ib):
            total = None
            for a in range(0, nl, 4):
                rows = jnp.concatenate([dense[lcol[s, b, a + i]] for i in range(4)], axis=0)
                term = jnp.dot(
                    lbuf[s, b * bs : (b + 1) * bs, a * bs : (a + 4) * bs], rows, preferred_element_type=jnp.float32
                )
                total = term if total is None else total + term
            for j in range(8):
                wide[b, j] = total[:, j * 2 * bs : (j + 1) * 2 * bs]
            for o in range(0, no, 2):
                j0 = ocol[s, b, o]
                j1 = ocol[s, b, o + 1]
                v0 = wide[b, j0 // 2]
                v1 = wide[b, j1 // 2]
                w0 = jnp.where(lax.rem(j0, 2) == 1, pltpu.roll(v0, bs, 1), v0)
                w1 = jnp.where(lax.rem(j1, 2) == 1, v1, pltpu.roll(v1, bs, 1))
                part[s, b * bs : (b + 1) * bs, o * bs : (o + 2) * bs] = jnp.where(low, w0, w1)

    def send_sum(s):
        return remote(
            part.at[s], acc.at[s], sum_send.at[s], sum_recv.at[s], {"col": lax.rem(col + 1, n_col)}
        )

    send_ocol(0).wait_recv()
    product(0)
    send_sum(0).start()

    to_far.wait_recv()
    for d in range(1, 4):
        @pl.when(y + d >= 4)
        def _():
            to_y(d, TICKS).start()

    @pl.when(core == 1)
    def _():
        to_sibling(3, TICKS, NEAR).start()

    for d in range(1, 4):
        to_y(d, 0).wait_recv()
        to_sibling(d - core, 2 * d, 2 * (d - core) + 1).start()

    def tick(s, carry):
        @pl.when(lax.rem(s, 2) == 1)
        def _():
            to_sibling(s // 2, 0, s).wait_recv()

        send_lcol(s).wait_recv()

        @pl.when(s < NEAR)
        def _():
            send_ocol(s).wait_recv()

        product(s)
        send_sum(s - 1).wait_recv()
        part[s] = part[s] + acc[s - 1]

        @pl.when(s < NEAR)
        def _():
            send_sum(s).start()

        return carry

    lax.fori_loop(1, TICKS, tick, 0)

    for b in range(ib):
        for o in range(no):
            out_ref[b, o] = part[NEAR, b * bs : (b + 1) * bs, o * bs : (o + 1) * bs]

    to_far.wait_send()
    for d in range(1, 4):
        to_y(d, 0).wait_send()
    for i in range(4):
        to_sibling(i, 0, 1).wait_send()
    for s in range(NEAR):
        send_ocol(s).wait_send()
        send_lcol(s + 1).wait_send()
        send_sum(s).wait_send()


def solution(mesh):
    n_row, n_col = mesh.shape["row"], mesh.shape["col"]

    def on_device(left_blocks, left_cols, right_blocks, right_cols, out_cols):
        left, right = left_blocks[0, 0], right_blocks[0, 0]
        left_cols, right_cols, out_cols = left_cols[0, 0], right_cols[0, 0], out_cols[0, 0]
        ib, nl, bs, _ = left.shape
        kb, nr = right_cols.shape
        no = out_cols.shape[1]
        dma = pltpu.SemaphoreType.DMA
        product = pl.pallas_call(
            functools.partial(kernel, n_row, n_col),
            out_shape=jax.ShapeDtypeStruct((ib, no, bs, bs), jnp.float32),
            in_specs=[
                pl.BlockSpec(memory_space=pl.ANY),
                pl.BlockSpec(memory_space=pltpu.SMEM),
                pl.BlockSpec(memory_space=pl.ANY),
                pl.BlockSpec(memory_space=pltpu.SMEM),
                pl.BlockSpec(memory_space=pltpu.SMEM),
            ],
            out_specs=pl.BlockSpec(memory_space=pltpu.VMEM),
            scratch_shapes=[
                pltpu.VMEM(left.shape, left.dtype),
                pltpu.VMEM((kb, nr + 1, bs, bs), right.dtype),
                pltpu.VMEM((TICKS + 1, ib * bs, nl * bs), left.dtype),
                pltpu.VMEM((kb, bs, 16 * bs), right.dtype),
                pltpu.VMEM((ib, 8, bs, 2 * bs), jnp.float32),
                pltpu.VMEM((TICKS, ib * bs, no * bs), jnp.float32),
                pltpu.VMEM((NEAR, ib * bs, no * bs), jnp.float32),
                pltpu.SMEM((TICKS, ib, nl), jnp.int32),
                pltpu.SMEM((TICKS, ib, no), jnp.int32),
                dma((2,)),
                dma((TICKS,)), dma((TICKS,)),
                dma((TICKS,)), dma((TICKS,)),
                dma, dma,
                dma((3,)), dma((3,)),
                dma((4,)), dma((4,)),
                dma((NEAR,)), dma((NEAR,)),
            ],
            compiler_params=pltpu.CompilerParams(collective_id=0, has_side_effects=True),
        )(left, left_cols, right, right_cols, out_cols)
        return product[None, None]

    blocks = P("row", "col", None, None, None, None)
    table = P("row", "col", None, None)
    return jax.shard_map(
        on_device,
        mesh=mesh,
        in_specs=(blocks, table, blocks, table, table),
        out_specs=blocks,
        check_vma=False,
    )
```

```python
import functools

import jax
import jax.numpy as jnp
from jax import lax
from jax.experimental import pallas as pl
from jax.experimental.pallas import tpu as pltpu
from jax.sharding import PartitionSpec as P

TICKS = 8
NEAR = TICKS - 1
LINE = 8
FULL = 32767.0
MESH = pl.DeviceIdType.MESH


def kernel(
    n_row, n_col, left_hbm, left_cols, right_hbm, right_cols, out_cols, out_ref,
    lraw, rraw, lbuf, dense, wide, part, sent, sent_scale, got, got_scale, lcol, ocol,
    local_sem, lc_send, lc_recv, oc_send, oc_recv, far_send, far_recv, y_send, y_recv, sib_send, sib_recv,
    sum_send, sum_recv, scale_send, scale_recv,
):
    row = lax.axis_index("row")
    col = lax.axis_index("col")
    y = lax.rem(row // 2, 4)
    half = row // 8
    core = lax.rem(row, 2)
    z = lax.rem(col, LINE)
    far = lax.rem(row + 8, n_row)
    sibling = row + 1 - 2 * core
    ib, nl, bs, _ = lraw.shape
    kb = rraw.shape[0]
    nr = rraw.shape[1] - 1
    no = ocol.shape[2]

    get_left = pltpu.make_async_copy(left_hbm, lraw, local_sem.at[0])
    get_right = pltpu.make_async_copy(right_hbm, rraw.at[:, pl.ds(0, nr)], local_sem.at[1])
    get_left.start()
    get_right.start()

    barrier = pltpu.get_barrier_semaphore()
    for d in range(1, n_row):
        pl.semaphore_signal(barrier, inc=1, device_id={"row": lax.rem(row + d, n_row)}, device_id_type=MESH)
    for d in range(1, TICKS):
        for e in (d, n_col - d):
            pl.semaphore_signal(barrier, inc=1, device_id={"col": lax.rem(col + e, n_col)}, device_id_type=MESH)

    def remote(src, dst, send, recv, to):
        return pltpu.make_async_remote_copy(
            src_ref=src, dst_ref=dst, send_sem=send, recv_sem=recv, device_id=to, device_id_type=MESH
        )

    get_left.wait()
    for b in range(ib):
        for a in range(0, nl, 2):
            lbuf[0, b, :, a * bs : (a + 2) * bs] = jnp.concatenate([lraw[b, a], lraw[b, a + 1]], axis=1)
    for b in range(ib):
        for a in range(nl):
            lcol[0, b, a] = left_cols[b, a]
        for o in range(no):
            ocol[NEAR, b, o] = out_cols[b, o]
    for i in range(kb):
        rraw[i, nr] = jnp.zeros((bs, bs), rraw.dtype)

    pl.semaphore_wait(barrier, n_row - 1 + 2 * NEAR)

    def send_ocol(s):
        return remote(out_cols, ocol.at[s], oc_send.at[s], oc_recv.at[s], {"col": lax.rem(col + n_col - NEAR + s, n_col)})

    def send_lcol(s):
        return remote(left_cols, lcol.at[s], lc_send.at[s], lc_recv.at[s], {"row": lax.rem(row + s, n_row)})

    def to_far(b):
        return remote(lbuf.at[0, b], lbuf.at[TICKS, b], far_send.at[b], far_recv.at[b], {"row": far})

    def to_y(d, src, b):
        return remote(
            lbuf.at[src, b], lbuf.at[2 * d, b], y_send.at[d - 1, b], y_recv.at[d - 1, b],
            {"row": half * 8 + lax.rem(y + d, 4) * 2 + core},
        )

    def to_sibling(i, src, dst, b):
        return remote(lbuf.at[src, b], lbuf.at[dst, b], sib_send.at[i, b], sib_recv.at[i, b], {"row": sibling})

    @pl.when(half == 1)
    def _():
        for b in range(ib):
            to_far(b).start()

    for d in range(1, 4):
        @pl.when(y + d < 4)
        def _():
            for b in range(ib):
                to_y(d, 0, b).start()

    @pl.when(core == 0)
    def _():
        for b in range(ib):
            to_sibling(0, 0, 1, b).start()

    for s in range(TICKS):
        if s < NEAR:
            send_ocol(s).start()
        if s > 0:
            send_lcol(s).start()

    get_right.wait()

    def fill(k, carry):
        cols = [right_cols[e, k] for e in range(nr)]

        def slot_of(j):
            slot = jnp.int32(nr)
            for e in range(nr):
                slot = jnp.where(cols[e] == j, e, slot)
            return slot

        for j in range(0, 16, 2):
            dense[k, :, j * bs : (j + 2) * bs] = jnp.concatenate(
                [rraw[k, slot_of(j)], rraw[k, slot_of(j + 1)]], axis=1
            )
        return carry

    lax.fori_loop(0, kb, fill, 0)

    for b in range(ib):
        to_far(b).wait_recv()

        @pl.when(half == 0)
        def _():
            to_far(b).start()

        for d in range(1, 4):
            @pl.when(y + d >= 4)
            def _():
                to_y(d, TICKS, b).start()

        @pl.when(core == 1)
        def _():
            to_sibling(3, TICKS, NEAR, b).start()

    for b in range(ib):
        for d in range(1, 4):
            to_y(d, 0, b).wait_recv()
            to_sibling(d - core, 2 * d, 2 * (d - core) + 1, b).start()

    low = lax.broadcasted_iota(jnp.int32, (bs, 2 * bs), 1) < bs

    def product(s):
        send_lcol_wait = s > 0

        @pl.when(send_lcol_wait)
        def _():
            send_lcol(s).wait_recv()

        @pl.when(s < NEAR)
        def _():
            send_ocol(s).wait_recv()

        for b in range(ib):
            @pl.when(lax.rem(s, 2) == 1)
            def _():
                to_sibling(s // 2, 0, s, b).wait_recv()

            total = None
            for a in range(0, nl, 4):
                rows = jnp.concatenate([dense[lcol[s, b, a + i]] for i in range(4)], axis=0)
                term = jnp.dot(lbuf[s, b, :, a * bs : (a + 4) * bs], rows, preferred_element_type=jnp.float32)
                total = term if total is None else total + term
            for j in range(8):
                wide[b, j] = total[:, j * 2 * bs : (j + 1) * 2 * bs]
            for o in range(0, no, 2):
                j0 = ocol[s, b, o]
                j1 = ocol[s, b, o + 1]
                v0 = wide[b, j0 // 2]
                v1 = wide[b, j1 // 2]
                w0 = jnp.where(lax.rem(j0, 2) == 1, pltpu.roll(v0, bs, 1), v0)
                w1 = jnp.where(lax.rem(j1, 2) == 1, v1, pltpu.roll(v1, bs, 1))
                part[s, b, :, o * bs : (o + 2) * bs] = jnp.where(low, w0, w1)

    def send_sum(s, slot, to, b):
        to = {"col": lax.rem(to, n_col)}
        return (
            remote(sent.at[s, b], got.at[slot, b], sum_send.at[s, b], sum_recv.at[slot, b], to),
            remote(sent_scale.at[s, b], got_scale.at[slot, b], scale_send.at[s, b], scale_recv.at[slot, b], to),
        )

    def receive(s, slot, b):
        for copy in send_sum(0, slot, col + 1, b):
            copy.wait_recv()
        part[s, b] = part[s, b] + got[slot, b].astype(jnp.float32) * got_scale[slot, b]

    def pass_on(s, slot, to, has_input):
        for b in range(ib):
            @pl.when(has_input)
            def _():
                receive(s, s, b)

            total = part[s, b]
            top = jnp.maximum(jnp.max(jnp.abs(total), axis=0, keepdims=True), 1e-30)
            sent[s, b] = jnp.round(total * (FULL / top)).astype(jnp.int32).astype(jnp.int16)
            sent_scale[s, b] = top * (1.0 / FULL)
            for copy in send_sum(s, slot, to, b):
                copy.start()

    def products(t):
        @pl.when(t >= z)
        def _():
            product(t)

        @pl.when((t >= LINE - 1 - z) & (t < NEAR))
        def _():
            product(NEAR - 1 - t)

    def step(t, carry):
        @pl.when(t >= z)
        def _():
            pass_on(t, t + 1, col + 1, z > 0)

        @pl.when(t >= LINE - 1 - z)
        def _():
            s = NEAR - 1 - t
            first = s == 0
            pass_on(
                s, jnp.where(first, TICKS, s - 1), jnp.where(first, col + LINE - 1, col + n_col - 1), z < LINE - 1
            )

        products(t + 1)
        return carry

    products(jnp.int32(0))
    lax.fori_loop(0, NEAR, step, 0)

    for b in range(ib):
        @pl.when(z > 0)
        def _():
            receive(NEAR, NEAR, b)

        @pl.when(z < LINE - 1)
        def _():
            receive(NEAR, TICKS, b)

        for o in range(no):
            out_ref[b, o] = part[NEAR, b, :, o * bs : (o + 1) * bs]

    for b in range(ib):
        to_far(b).wait_send()
        for d in range(1, 4):
            to_y(d, 0, b).wait_send()
        for i in range(4):
            to_sibling(i, 0, 1, b).wait_send()
        for s in range(NEAR):
            for copy in send_sum(s, 0, col + 1, b):
                copy.wait_send()
    for s in range(NEAR):
        send_ocol(s).wait_send()
        send_lcol(s + 1).wait_send()


def solution(mesh):
    n_row, n_col = mesh.shape["row"], mesh.shape["col"]

    def on_device(left_blocks, left_cols, right_blocks, right_cols, out_cols):
        left, right = left_blocks[0, 0], right_blocks[0, 0]
        left_cols, right_cols, out_cols = left_cols[0, 0], right_cols[0, 0].T, out_cols[0, 0]
        ib, nl, bs, _ = left.shape
        nr, kb = right_cols.shape
        no = out_cols.shape[1]
        dma = pltpu.SemaphoreType.DMA
        product = pl.pallas_call(
            functools.partial(kernel, n_row, n_col),
            out_shape=jax.ShapeDtypeStruct((ib, no, bs, bs), jnp.float32),
            in_specs=[
                pl.BlockSpec(memory_space=pl.ANY),
                pl.BlockSpec(memory_space=pltpu.SMEM),
                pl.BlockSpec(memory_space=pl.ANY),
                pl.BlockSpec(memory_space=pltpu.SMEM),
                pl.BlockSpec(memory_space=pltpu.SMEM),
            ],
            out_specs=pl.BlockSpec(memory_space=pltpu.VMEM),
            scratch_shapes=[
                pltpu.VMEM(left.shape, left.dtype),
                pltpu.VMEM((kb, nr + 1, bs, bs), right.dtype),
                pltpu.VMEM((TICKS + 1, ib, bs, nl * bs), left.dtype),
                pltpu.VMEM((kb, bs, 16 * bs), right.dtype),
                pltpu.VMEM((ib, 8, bs, 2 * bs), jnp.float32),
                pltpu.VMEM((TICKS, ib, bs, no * bs), jnp.float32),
                pltpu.VMEM((NEAR, ib, bs, no * bs), jnp.int16),
                pltpu.VMEM((NEAR, ib, 1, no * bs), jnp.float32),
                pltpu.VMEM((TICKS + 1, ib, bs, no * bs), jnp.int16),
                pltpu.VMEM((TICKS + 1, ib, 1, no * bs), jnp.float32),
                pltpu.SMEM((TICKS, ib, nl), jnp.int32),
                pltpu.SMEM((TICKS, ib, no), jnp.int32),
                dma((2,)),
                dma((TICKS,)), dma((TICKS,)),
                dma((TICKS,)), dma((TICKS,)),
                dma((ib,)), dma((ib,)),
                dma((3, ib)), dma((3, ib)),
                dma((4, ib)), dma((4, ib)),
                dma((NEAR, ib)), dma((TICKS + 1, ib)),
                dma((NEAR, ib)), dma((TICKS + 1, ib)),
            ],
            compiler_params=pltpu.CompilerParams(collective_id=0, has_side_effects=True),
        )(left, left_cols, right, right_cols, out_cols)
        return product[None, None]

    blocks = P("row", "col", None, None, None, None)
    table = P("row", "col", None, None)
    return jax.shard_map(
        on_device,
        mesh=mesh,
        in_specs=(blocks, table, blocks, table, table),
        out_specs=blocks,
        check_vma=False,
    )
```

```python
import functools

import jax
import jax.numpy as jnp
from jax import lax
from jax.experimental import pallas as pl
from jax.experimental.pallas import tpu as pltpu
from jax.sharding import PartitionSpec as P

TICKS = 8
NEAR = TICKS - 1
LINE = 8
FULL = 32767.0
SUB = 2
MESH = pl.DeviceIdType.MESH


def kernel(
    n_row, n_col, left_hbm, left_cols, right_hbm, right_cols, out_cols, out_ref,
    lraw, rraw, lbuf, dense, wide, part, sent, sent_scale, got, got_scale, lcol, ocol,
    local_sem, oc_send, oc_recv, far_send, far_recv, y_send, y_recv, sib_send, sib_recv,
    sum_send, sum_recv, scale_send, scale_recv, far_ready,
):
    row = lax.axis_index("row")
    col = lax.axis_index("col")
    y = lax.rem(row // 2, 4)
    half = row // 8
    core = lax.rem(row, 2)
    z = lax.rem(col, LINE)
    line = col - z
    far = lax.rem(row + 8, n_row)
    sibling = row + 1 - 2 * core
    ib, nl, bs, _ = lraw.shape
    kb = rraw.shape[0]
    nr = rraw.shape[1] - 1
    no = ocol.shape[2]
    sub = bs // SUB

    get_left = pltpu.make_async_copy(left_hbm, lraw, local_sem.at[0])
    get_right = pltpu.make_async_copy(right_hbm, rraw.at[:, pl.ds(0, nr)], local_sem.at[1])
    get_left.start()
    get_right.start()

    barrier = pltpu.get_barrier_semaphore()

    def greet(to):
        pl.semaphore_signal(barrier, inc=1, device_id=to, device_id_type=MESH)

    def y_row(d):
        return half * 8 + lax.rem(y + d, 4) * 2 + core

    def apart(n):
        return line + z + n - 2 * n * lax.rem(z // n, 2)

    @pl.when(half == 0)
    def _():
        greet({"row": far})

    greet({"row": sibling})
    for d in range(1, 4):
        greet({"row": y_row(d)})
    for n in (1, 2, 4):
        greet({"col": apart(n)})
    for d in (LINE, n_col - LINE):
        greet({"col": lax.rem(col + d, n_col)})
    inside = (z > 0) & (z < LINE - 1)

    @pl.when(inside)
    def _():
        greet({"col": line + z - 1 + 2 * lax.rem(z, 2)})

    @pl.when(z > 0)
    def _():
        greet({"col": lax.rem(col + LINE - 1, n_col)})

    @pl.when(z < LINE - 1)
    def _():
        greet({"col": lax.rem(col + n_col - LINE + 1, n_col)})

    def remote(src, dst, send, recv, to):
        return pltpu.make_async_remote_copy(
            src_ref=src, dst_ref=dst, send_sem=send, recv_sem=recv, device_id=to, device_id_type=MESH
        )

    get_left.wait()
    for b in range(ib):
        for a in range(0, nl, 2):
            lbuf[0, b, :, a * bs : (a + 2) * bs] = jnp.concatenate([lraw[b, a], lraw[b, a + 1]], axis=1)
    for b in range(ib):
        for a in range(nl):
            lcol[0, b, a] = left_cols[b, a]
        for o in range(no):
            ocol[z, b, o] = out_cols[b, o]
    for i in range(kb):
        rraw[i, nr] = jnp.zeros((bs, bs), rraw.dtype)

    pl.semaphore_wait(barrier, jnp.where(inside, 12, 10) + half)

    def panel(src, dst, send, recv, to, b):
        copies = [remote(lbuf.at[src, b], lbuf.at[dst, b], send.at[b], recv.at[b], to)]
        if b == 0:
            copies.append(remote(lcol.at[src], lcol.at[dst], send.at[ib], recv.at[ib], to))
        return copies

    def to_far(b):
        return panel(0, TICKS, far_send, far_recv, {"row": far}, b)

    def to_y(d, src, b):
        return panel(src, 2 * d, y_send.at[d - 1], y_recv.at[d - 1], {"row": y_row(d)}, b)

    def to_sibling(i, src, dst, b):
        return panel(src, dst, sib_send.at[i], sib_recv.at[i], {"row": sibling}, b)

    def start(copies):
        for copy in copies:
            copy.start()

    def wait_recv(copies):
        for copy in copies:
            copy.wait_recv()

    def wait_send(copies):
        for copy in copies:
            copy.wait_send()

    def to_apart(i):
        n = 1 << i
        mine = pl.ds(z // n * n, n)
        return remote(ocol.at[mine], ocol.at[mine], oc_send.at[i], oc_recv.at[i], {"col": apart(n)})

    to_line = remote(
        ocol.at[pl.ds(0, LINE)], ocol.at[pl.ds(LINE, LINE)], oc_send.at[3], oc_recv.at[3],
        {"col": lax.rem(col + n_col - LINE, n_col)},
    )

    @pl.when(half == 1)
    def _():
        pl.semaphore_signal(far_ready, inc=1, device_id={"row": far}, device_id_type=MESH)
        start(to_far(0))

    to_apart(0).start()
    for b in range(ib):
        for d in range(1, 4):
            @pl.when(y + d < 4)
            def _():
                start(to_y(d, 0, b))

    @pl.when(core == 0)
    def _():
        for b in range(ib):
            start(to_sibling(0, 0, 1, b))

    get_right.wait()

    def fill(k, carry):
        cols = [right_cols[0, e, 0, k] for e in range(nr)]

        def slot_of(j):
            slot = jnp.int32(nr)
            for e in range(nr):
                slot = jnp.where(cols[e] == j, e, slot)
            return slot

        for j in range(0, 16, 2):
            dense[k, :, j * bs : (j + 2) * bs] = jnp.concatenate(
                [rraw[k, slot_of(j)], rraw[k, slot_of(j + 1)]], axis=1
            )
        return carry

    lax.fori_loop(0, kb // 2, fill, 0)

    @pl.when(half == 1)
    def _():
        start(to_far(1))

    to_apart(0).wait_recv()
    to_apart(1).start()
    lax.fori_loop(kb // 2, kb, fill, 0)
    to_apart(1).wait_recv()
    to_apart(2).start()
    to_apart(2).wait_recv()
    to_line.start()

    low = lax.broadcasted_iota(jnp.int32, (bs, 2 * bs), 1) < bs

    def product(s, b, u):
        target = z + NEAR - s
        total = None
        for a in range(0, nl, 4):
            rows = jnp.concatenate([dense[lcol[s, b, a + n]] for n in range(4)], axis=0)
            term = jnp.dot(lbuf[s, b, :, a * bs : (a + 4) * bs], rows, preferred_element_type=jnp.float32)
            total = term if total is None else total + term
        for j in range(8):
            wide[u, j] = total[:, j * 2 * bs : (j + 1) * 2 * bs]
        for o in range(0, no, 2):
            j0 = ocol[target, b, o]
            j1 = ocol[target, b, o + 1]
            v0 = wide[u, j0 // 2]
            v1 = wide[u, j1 // 2]
            w0 = jnp.where(lax.rem(j0, 2) == 1, pltpu.roll(v0, bs, 1), v0)
            w1 = jnp.where(lax.rem(j1, 2) == 1, v1, pltpu.roll(v1, bs, 1))
            both = jnp.where(low, w0, w1)
            for h in range(SUB):
                part[s, b * SUB + h, :, o * bs : (o + 2) * bs] = both[h * sub : (h + 1) * sub]

    def send_sum(s, slot, to, g):
        to = {"col": lax.rem(to, n_col)}
        return (
            remote(sent.at[s, g], got.at[slot, g], sum_send.at[s, g], sum_recv.at[slot, g], to),
            remote(sent_scale.at[s, g], got_scale.at[slot, g], scale_send.at[s, g], scale_recv.at[slot, g], to),
        )

    def receive(s, slot, g):
        wait_recv(send_sum(0, slot, col + 1, g))
        part[s, g] = part[s, g] + got[slot, g].astype(jnp.float32) * got_scale[slot, g]

    def pass_on(s, slot, to, has_input, g):
        @pl.when(has_input)
        def _():
            receive(s, s, g)

        total = part[s, g]
        top = jnp.maximum(jnp.max(jnp.abs(total), axis=0, keepdims=True), 1e-30)
        sent[s, g] = jnp.round(total * (FULL / top)).astype(jnp.int32).astype(jnp.int16)
        sent_scale[s, g] = top * (1.0 / FULL)
        start(send_sum(s, slot, to, g))

    def step(t, b):
        chunks = range(b * SUB, (b + 1) * SUB)

        @pl.when((t >= z) & (t > 0))
        def _():
            for g in chunks:
                pass_on(t, t + 1, col + 1, z > 0, g)

        @pl.when((t >= LINE - 1 - z) & ((t < NEAR - 1) | (z < LINE - 1)))
        def _():
            s = NEAR - 1 - t
            first = s == 0
            slot = jnp.where(first, TICKS, s - 1)
            to = jnp.where(first, col + LINE - 1, col + n_col - 1)
            for g in chunks:
                pass_on(s, slot, to, z < LINE - 1, g)

    def products(i, b):
        if i < 4:
            product(i, b, 0)
            product(NEAR - i, b, 1)
        else:
            product(NEAR, b, 0)

    def from_far(b):
        wait_recv(to_far(b))
        for d in range(1, 4):
            @pl.when(y + d >= 4)
            def _():
                start(to_y(d, TICKS, b))

        @pl.when(core == 1)
        def _():
            start(to_sibling(3, TICKS, NEAR, b))

    def collect(b):
        for d in range(1, 4):
            wait_recv(to_y(d, 0, b))
            start(to_sibling(d - core, 2 * d, 2 * (d - core) + 1, b))

    def from_sibling(b):
        for i in range(4):
            wait_recv(to_sibling(i, 0, 1, b))

    to_line.wait_recv()
    for b in range(ib):
        product(0, b, b)

    @pl.when(z == 0)
    def _():
        for g in range(ib * SUB):
            pass_on(0, 1, col + 1, z > 0, g)

    @pl.when(z == LINE - 1)
    def _():
        for g in range(ib * SUB):
            pass_on(0, TICKS, col + LINE - 1, z < LINE - 1, g)

    @pl.when(half == 0)
    def _():
        pl.semaphore_wait(far_ready, 1)
        start(to_far(0))

    from_far(0)
    collect(0)

    @pl.when(half == 0)
    def _():
        start(to_far(1))

    from_far(1)
    from_sibling(0)
    products(1, 0)
    step(jnp.int32(0), 0)
    products(2, 0)
    step(jnp.int32(1), 0)
    collect(1)
    products(3, 0)
    products(4, 0)
    from_sibling(1)
    products(1, 1)
    step(jnp.int32(0), 1)
    products(2, 1)
    step(jnp.int32(1), 1)
    products(3, 1)
    products(4, 1)

    def steps(t, carry):
        for b in range(ib):
            step(t, b)
        return carry

    lax.fori_loop(2, NEAR, steps, 0)

    for g in range(ib * SUB):
        @pl.when(z > 0)
        def _():
            receive(NEAR, NEAR, g)

        @pl.when(z < LINE - 1)
        def _():
            receive(NEAR, TICKS, g)

        for o in range(no):
            out_ref[g // SUB, o, g % SUB * sub : (g % SUB + 1) * sub] = part[NEAR, g, :, o * bs : (o + 1) * bs]

    for b in range(ib):
        wait_send(to_far(b))
        for d in range(1, 4):
            wait_send(to_y(d, 0, b))
        for i in range(4):
            wait_send(to_sibling(i, 0, 1, b))
    for s in range(NEAR):
        for g in range(ib * SUB):
            wait_send(send_sum(s, 0, col + 1, g))
    for i in range(3):
        to_apart(i).wait_send()
    to_line.wait_send()


def solution(mesh):
    n_row, n_col = mesh.shape["row"], mesh.shape["col"]

    def on_device(left_blocks, left_cols, right_blocks, right_cols, out_cols):
        left, right = left_blocks[0, 0], right_blocks[0, 0]
        left_cols, right_cols, out_cols = left_cols[0, 0], lax.transpose(right_cols, (0, 3, 1, 2)), out_cols[0, 0]
        ib, nl, bs, _ = left.shape
        _, nr, _, kb = right_cols.shape
        no = out_cols.shape[1]
        dma = pltpu.SemaphoreType.DMA
        product = pl.pallas_call(
            functools.partial(kernel, n_row, n_col),
            out_shape=jax.ShapeDtypeStruct((ib, no, bs, bs), jnp.float32),
            in_specs=[
                pl.BlockSpec(memory_space=pl.ANY),
                pl.BlockSpec(memory_space=pltpu.SMEM),
                pl.BlockSpec(memory_space=pl.ANY),
                pl.BlockSpec(memory_space=pltpu.SMEM),
                pl.BlockSpec(memory_space=pltpu.SMEM),
            ],
            out_specs=pl.BlockSpec(memory_space=pltpu.VMEM),
            scratch_shapes=[
                pltpu.VMEM(left.shape, left.dtype),
                pltpu.VMEM((kb, nr + 1, bs, bs), right.dtype),
                pltpu.VMEM((TICKS + 1, ib, bs, nl * bs), left.dtype),
                pltpu.VMEM((kb, bs, 16 * bs), right.dtype),
                pltpu.VMEM((ib, 8, bs, 2 * bs), jnp.float32),
                pltpu.VMEM((TICKS, ib * SUB, bs // SUB, no * bs), jnp.float32),
                pltpu.VMEM((NEAR, ib * SUB, bs // SUB, no * bs), jnp.int16),
                pltpu.VMEM((NEAR, ib * SUB, 1, no * bs), jnp.float32),
                pltpu.VMEM((TICKS + 1, ib * SUB, bs // SUB, no * bs), jnp.int16),
                pltpu.VMEM((TICKS + 1, ib * SUB, 1, no * bs), jnp.float32),
                pltpu.SMEM((TICKS + 1, ib, nl), jnp.int32),
                pltpu.SMEM((2 * LINE, ib, no), jnp.int32),
                dma((2,)),
                dma((4,)), dma((4,)),
                dma((ib + 1,)), dma((ib + 1,)),
                dma((3, ib + 1)), dma((3, ib + 1)),
                dma((4, ib + 1)), dma((4, ib + 1)),
                dma((NEAR, ib * SUB)), dma((TICKS + 1, ib * SUB)),
                dma((NEAR, ib * SUB)), dma((TICKS + 1, ib * SUB)),
                pltpu.SemaphoreType.REGULAR,
            ],
            compiler_params=pltpu.CompilerParams(collective_id=0, has_side_effects=True),
        )(left, left_cols, right, right_cols, out_cols)
        return product[None, None]

    blocks = P("row", "col", None, None, None, None)
    table = P("row", "col", None, None)
    return jax.shard_map(
        on_device,
        mesh=mesh,
        in_specs=(blocks, table, blocks, table, table),
        out_specs=blocks,
        check_vma=False,
    )
```

```python
import functools

import jax
import jax.numpy as jnp
from jax import lax
from jax.experimental import pallas as pl
from jax.experimental.pallas import tpu as pltpu
from jax.sharding import PartitionSpec as P

TICKS = 8
NEAR = TICKS - 1
LINE = 8
QUAD = 4
FULL = 32767.0
SUB = 2
MESH = pl.DeviceIdType.MESH


def kernel(
    n_row, n_col, left_hbm, left_cols, right_hbm, right_cols, out_cols, out_ref,
    lraw, rraw, lbuf, dense, wide, part, sent, sent_scale, got, got_scale, lcol, ocol,
    local_sem, oc_send, oc_recv, far_send, far_recv, y_send, y_recv, sib_send, sib_recv,
    sum_send, sum_recv, scale_send, scale_recv, far_ready,
):
    row = lax.axis_index("row")
    col = lax.axis_index("col")
    y = lax.rem(row // 2, 4)
    half = row // 8
    core = lax.rem(row, 2)
    z = lax.rem(col, LINE)
    line = col - z
    upper = z // QUAD
    place = lax.rem(z, QUAD)
    far = lax.rem(row + 8, n_row)
    sibling = row + 1 - 2 * core
    ib, nl, bs, _ = lraw.shape
    kb = rraw.shape[0]
    nr = rraw.shape[1] - 1
    no = ocol.shape[2]
    sub = bs // SUB

    get_left = pltpu.make_async_copy(left_hbm, lraw, local_sem.at[0])
    get_right = pltpu.make_async_copy(right_hbm, rraw.at[:, pl.ds(0, nr)], local_sem.at[1])
    get_left.start()
    get_right.start()

    barrier = pltpu.get_barrier_semaphore()

    def greet(to):
        pl.semaphore_signal(barrier, inc=1, device_id=to, device_id_type=MESH)

    def y_row(d):
        return half * 8 + lax.rem(y + d, 4) * 2 + core

    @pl.when(half == 0)
    def _():
        greet({"row": far})

    greet({"row": sibling})
    for d in range(1, 4):
        greet({"row": y_row(d)})
    for i in range(1, QUAD):
        greet({"col": line + QUAD * upper + lax.rem(place + i, QUAD)})
    ahead = lax.rem(col + LINE, n_col)
    greet({"col": ahead})

    greet({"col": jnp.where(upper == 1, ahead - QUAD, col + QUAD)})

    @pl.when(place < QUAD - 1)
    def _():
        greet({"col": lax.rem(col + n_col - LINE + 1, n_col)})

    @pl.when(upper == 1)
    def _():
        greet({"col": line + QUAD - 1})

    @pl.when(upper == 0)
    def _():
        greet({"col": lax.rem(col + n_col - QUAD - z, n_col)})

    n_greeted = 9 + half + jnp.where(z == 0, 0, jnp.where(z == QUAD - 1, 5, jnp.where(z == QUAD, 4, 1)))

    def remote(src, dst, send, recv, to):
        return pltpu.make_async_remote_copy(
            src_ref=src, dst_ref=dst, send_sem=send, recv_sem=recv, device_id=to, device_id_type=MESH
        )

    get_left.wait()
    for b in range(ib):
        for a in range(0, nl, 2):
            lbuf[0, b, :, a * bs : (a + 2) * bs] = jnp.concatenate([lraw[b, a], lraw[b, a + 1]], axis=1)
    for b in range(ib):
        for a in range(nl):
            lcol[0, b, a] = left_cols[b, a]
        for o in range(no):
            ocol[z, b, o] = out_cols[b, o]
    for i in range(kb):
        rraw[i, nr] = jnp.zeros((bs, bs), rraw.dtype)

    pl.semaphore_wait(barrier, n_greeted)

    def panel(src, dst, send, recv, to, b):
        copies = [remote(lbuf.at[src, b], lbuf.at[dst, b], send.at[b], recv.at[b], to)]
        if b == 0:
            copies.append(remote(lcol.at[src], lcol.at[dst], send.at[ib], recv.at[ib], to))
        return copies

    def to_far(b):
        return panel(0, TICKS, far_send, far_recv, {"row": far}, b)

    def to_y(d, src, b):
        return panel(src, 2 * d, y_send.at[d - 1], y_recv.at[d - 1], {"row": y_row(d)}, b)

    def to_sibling(i, src, dst, b):
        return panel(src, dst, sib_send.at[i], sib_recv.at[i], {"row": sibling}, b)

    def start(copies):
        for copy in copies:
            copy.start()

    def wait_recv(copies):
        for copy in copies:
            copy.wait_recv()

    def wait_send(copies):
        for copy in copies:
            copy.wait_send()

    def to_mate(i):
        return remote(
            out_cols, ocol.at[z], oc_send.at[i - 1], oc_recv.at[i - 1], {"col": line + QUAD * upper + lax.rem(place + i, QUAD)}
        )

    def from_mate(i):
        return remote(
            out_cols, ocol.at[QUAD * upper + lax.rem(place + QUAD - i, QUAD)], oc_send.at[i - 1], oc_recv.at[i - 1],
            {"col": line + QUAD * upper + lax.rem(place + QUAD - i, QUAD)},
        )

    quad = pl.ds(QUAD * upper, QUAD)
    back = pl.ds(LINE + QUAD * upper, QUAD)
    low_back = pl.ds(jnp.where(upper == 1, QUAD, LINE), QUAD)
    behind = lax.rem(col + n_col - LINE, n_col)
    to_behind = remote(ocol.at[quad], ocol.at[back], oc_send.at[3], oc_recv.at[3], {"col": behind})
    to_other = remote(
        ocol.at[quad], ocol.at[low_back], oc_send.at[4], oc_recv.at[4], {"col": jnp.where(upper == 1, col - QUAD, behind + QUAD)}
    )

    @pl.when(half == 1)
    def _():
        pl.semaphore_signal(far_ready, inc=1, device_id={"row": far}, device_id_type=MESH)
        start(to_far(0))

    for i in range(1, QUAD):
        to_mate(i).start()
    for b in range(ib):
        for d in range(1, 4):
            @pl.when(y + d < 4)
            def _():
                start(to_y(d, 0, b))

    @pl.when(core == 0)
    def _():
        for b in range(ib):
            start(to_sibling(0, 0, 1, b))

    get_right.wait()

    def fill(k, carry):
        cols = [right_cols[0, e, 0, k] for e in range(nr)]

        def slot_of(j):
            slot = jnp.int32(nr)
            for e in range(nr):
                slot = jnp.where(cols[e] == j, e, slot)
            return slot

        for j in range(0, 16, 2):
            dense[k, :, j * bs : (j + 2) * bs] = jnp.concatenate(
                [rraw[k, slot_of(j)], rraw[k, slot_of(j + 1)]], axis=1
            )
        return carry

    lax.fori_loop(0, kb // 2, fill, 0)

    @pl.when(half == 1)
    def _():
        start(to_far(1))

    lax.fori_loop(kb // 2, kb, fill, 0)
    for i in range(1, QUAD):
        from_mate(i).wait_recv()
    to_behind.start()
    to_other.start()

    @pl.when(half == 0)
    def _():
        pl.semaphore_wait(far_ready, 1)
        for b in range(ib):
            start(to_far(b))

    low = lax.broadcasted_iota(jnp.int32, (bs, 2 * bs), 1) < bs

    def product(s, b, u):
        target = z + NEAR - s
        total = None
        for a in range(0, nl, 4):
            rows = jnp.concatenate([dense[lcol[s, b, a + n]] for n in range(4)], axis=0)
            term = jnp.dot(lbuf[s, b, :, a * bs : (a + 4) * bs], rows, preferred_element_type=jnp.float32)
            total = term if total is None else total + term
        for j in range(8):
            wide[u, j] = total[:, j * 2 * bs : (j + 1) * 2 * bs]
        for o in range(0, no, 2):
            j0 = ocol[target, b, o]
            j1 = ocol[target, b, o + 1]
            v0 = wide[u, j0 // 2]
            v1 = wide[u, j1 // 2]
            w0 = jnp.where(lax.rem(j0, 2) == 1, pltpu.roll(v0, bs, 1), v0)
            w1 = jnp.where(lax.rem(j1, 2) == 1, v1, pltpu.roll(v1, bs, 1))
            both = jnp.where(low, w0, w1)
            for h in range(SUB):
                part[s, b * SUB + h, :, o * bs : (o + 2) * bs] = both[h * sub : (h + 1) * sub]

    def send_sum(s, slot, to, g):
        to = {"col": lax.rem(to, n_col)}
        return (
            remote(sent.at[s, g], got.at[slot, g], sum_send.at[s, g], sum_recv.at[slot, g], to),
            remote(sent_scale.at[s, g], got_scale.at[slot, g], scale_send.at[s, g], scale_recv.at[slot, g], to),
        )

    def receive(s, slot, g):
        wait_recv(send_sum(0, slot, col + 1, g))
        part[s, g] = part[s, g] + got[slot, g].astype(jnp.float32) * got_scale[slot, g]

    def pass_on(s, slot, to, has_input, g):
        @pl.when(has_input)
        def _():
            receive(s, s, g)

        total = part[s, g]
        top = jnp.maximum(jnp.max(jnp.abs(total), axis=0, keepdims=True), 1e-30)
        sums, scales = send_sum(s, slot, to, g)
        sent_scale[s, g] = top * (1.0 / FULL)
        scales.start()
        sent[s, g] = jnp.round(total * (FULL / top)).astype(jnp.int32).astype(jnp.int16)
        sums.start()

    def up(s, g):
        last = z == QUAD - 1
        pass_on(
            s, jnp.where(last, TICKS + 1, s + 1), jnp.where(last, col + NEAR - s, col + 1), place > 0, g
        )

    def down(s, g):
        across = z == QUAD
        ends = across | (s == 0)
        pass_on(
            s,
            jnp.where(across, TICKS + 2, jnp.where(ends, TICKS, s - 1)),
            jnp.where(ends, col + NEAR - s, col + n_col - 1),
            place < QUAD - 1,
            g,
        )

    def step(t, b):
        chunks = range(b * SUB, (b + 1) * SUB)
        s_up = t + QUAD * upper
        s_down = 2 + QUAD * upper - t

        @pl.when((t >= place) & (s_up < NEAR) & (s_up > 0))
        def _():
            for g in chunks:
                up(s_up, g)

        @pl.when((s_down >= 0) & (s_down < z) & ((s_down > 0) | (place < QUAD - 1)))
        def _():
            for g in chunks:
                down(s_down, g)

    def products(i, b):
        if i < 3:
            product(jnp.where(upper == 1, (4, 5, 2)[i], (1, 3, 5)[i]), b, 0)
            product(jnp.where(upper == 1, (6, 3, 1)[i], (2, 4, 6)[i]), b, 1)
        else:
            product(NEAR, b, 0)

    def from_far(b):
        wait_recv(to_far(b))
        for d in range(1, 4):
            @pl.when(y + d >= 4)
            def _():
                start(to_y(d, TICKS, b))

        @pl.when(core == 1)
        def _():
            start(to_sibling(3, TICKS, NEAR, b))

    def collect(b):
        for d in range(1, 4):
            wait_recv(to_y(d, 0, b))
            start(to_sibling(d - core, 2 * d, 2 * (d - core) + 1, b))

    def from_sibling(b):
        for i in range(4):
            wait_recv(to_sibling(i, 0, 1, b))

    to_behind.wait_recv()
    to_other.wait_recv()
    for b in range(ib):
        product(0, b, b)

    @pl.when(z == 0)
    def _():
        for g in range(ib * SUB):
            up(0, g)

    @pl.when(place == QUAD - 1)
    def _():
        for g in range(ib * SUB):
            down(0, g)

    from_far(0)
    collect(0)
    from_far(1)
    from_sibling(0)
    products(0, 0)
    step(jnp.int32(0), 0)
    products(1, 0)
    step(jnp.int32(1), 0)
    collect(1)
    products(2, 0)
    products(3, 0)
    from_sibling(1)
    products(0, 1)
    step(jnp.int32(0), 1)
    products(1, 1)
    step(jnp.int32(1), 1)
    products(2, 1)
    products(3, 1)

    def steps(t, carry):
        for b in range(ib):
            step(t, b)
        return carry

    lax.fori_loop(2, NEAR, steps, 0)

    for g in range(ib * SUB):
        @pl.when(place > 0)
        def _():
            receive(NEAR, NEAR, g)

        @pl.when(place < QUAD - 1)
        def _():
            receive(NEAR, TICKS, g)

        receive(NEAR, TICKS + 2 - upper, g)

        for o in range(no):
            out_ref[g // SUB, o, g % SUB * sub : (g % SUB + 1) * sub] = part[NEAR, g, :, o * bs : (o + 1) * bs]

    for b in range(ib):
        wait_send(to_far(b))
        for d in range(1, 4):
            wait_send(to_y(d, 0, b))
        for i in range(4):
            wait_send(to_sibling(i, 0, 1, b))
    for s in range(NEAR):
        for g in range(ib * SUB):
            wait_send(send_sum(s, 0, col + 1, g))
    for i in range(1, QUAD):
        to_mate(i).wait_send()
    to_behind.wait_send()
    to_other.wait_send()


def solution(mesh):
    n_row, n_col = mesh.shape["row"], mesh.shape["col"]

    def on_device(left_blocks, left_cols, right_blocks, right_cols, out_cols):
        left, right = left_blocks[0, 0], right_blocks[0, 0]
        left_cols, right_cols, out_cols = left_cols[0, 0], lax.transpose(right_cols, (0, 3, 1, 2)), out_cols[0, 0]
        ib, nl, bs, _ = left.shape
        _, nr, _, kb = right_cols.shape
        no = out_cols.shape[1]
        dma = pltpu.SemaphoreType.DMA
        product = pl.pallas_call(
            functools.partial(kernel, n_row, n_col),
            out_shape=jax.ShapeDtypeStruct((ib, no, bs, bs), jnp.float32),
            in_specs=[
                pl.BlockSpec(memory_space=pl.ANY),
                pl.BlockSpec(memory_space=pltpu.SMEM),
                pl.BlockSpec(memory_space=pl.ANY),
                pl.BlockSpec(memory_space=pltpu.SMEM),
                pl.BlockSpec(memory_space=pltpu.SMEM),
            ],
            out_specs=pl.BlockSpec(memory_space=pltpu.VMEM),
            scratch_shapes=[
                pltpu.VMEM(left.shape, left.dtype),
                pltpu.VMEM((kb, nr + 1, bs, bs), right.dtype),
                pltpu.VMEM((TICKS + 1, ib, bs, nl * bs), left.dtype),
                pltpu.VMEM((kb, bs, 16 * bs), right.dtype),
                pltpu.VMEM((ib, 8, bs, 2 * bs), jnp.float32),
                pltpu.VMEM((TICKS, ib * SUB, bs // SUB, no * bs), jnp.float32),
                pltpu.VMEM((NEAR, ib * SUB, bs // SUB, no * bs), jnp.int16),
                pltpu.VMEM((NEAR, ib * SUB, 1, no * bs), jnp.float32),
                pltpu.VMEM((TICKS + 3, ib * SUB, bs // SUB, no * bs), jnp.int16),
                pltpu.VMEM((TICKS + 3, ib * SUB, 1, no * bs), jnp.float32),
                pltpu.SMEM((TICKS + 1, ib, nl), jnp.int32),
                pltpu.SMEM((2 * LINE, ib, no), jnp.int32),
                dma((2,)),
                dma((5,)), dma((5,)),
                dma((ib + 1,)), dma((ib + 1,)),
                dma((3, ib + 1)), dma((3, ib + 1)),
                dma((4, ib + 1)), dma((4, ib + 1)),
                dma((NEAR, ib * SUB)), dma((TICKS + 3, ib * SUB)),
                dma((NEAR, ib * SUB)), dma((TICKS + 3, ib * SUB)),
                pltpu.SemaphoreType.REGULAR,
            ],
            compiler_params=pltpu.CompilerParams(collective_id=0, has_side_effects=True),
        )(left, left_cols, right, right_cols, out_cols)
        return product[None, None]

    blocks = P("row", "col", None, None, None, None)
    table = P("row", "col", None, None)
    return jax.shard_map(
        on_device,
        mesh=mesh,
        in_specs=(blocks, table, blocks, table, table),
        out_specs=blocks,
        check_vma=False,
    )
```

```python
import functools

import jax
import jax.numpy as jnp
from jax import lax
from jax.experimental import pallas as pl
from jax.experimental.pallas import tpu as pltpu
from jax.sharding import PartitionSpec as P

TICKS = 8
NEAR = TICKS - 1
LINE = 8
QUAD = 4
FULL = 32767.0
SUB = 1
MESH = pl.DeviceIdType.MESH


def kernel(
    n_row, n_col, left_hbm, left_cols, right_hbm, right_cols, out_cols, out_ref,
    lraw, rraw, lbuf, dense, wide, part, sent, sent_scale, got, got_scale, lcol, ocol,
    local_sem, oc_send, oc_recv, far_send, far_recv, y_send, y_recv, sib_send, sib_recv,
    sum_send, sum_recv, scale_send, scale_recv, far_ready,
):
    row = lax.axis_index("row")
    col = lax.axis_index("col")
    y = lax.rem(row // 2, 4)
    half = row // 8
    core = lax.rem(row, 2)
    z = lax.rem(col, LINE)
    line = col - z
    upper = z // QUAD
    place = lax.rem(z, QUAD)
    far = lax.rem(row + 8, n_row)
    sibling = row + 1 - 2 * core
    ib, nl, bs, _ = lraw.shape
    kb = rraw.shape[0]
    nr = rraw.shape[1] - 1
    no = ocol.shape[2]
    sub = bs // SUB

    get_left = pltpu.make_async_copy(left_hbm, lraw, local_sem.at[0])
    get_right = pltpu.make_async_copy(right_hbm, rraw.at[:, pl.ds(0, nr)], local_sem.at[1])
    get_left.start()
    get_right.start()

    barrier = pltpu.get_barrier_semaphore()

    def greet(to):
        pl.semaphore_signal(barrier, inc=1, device_id=to, device_id_type=MESH)

    def y_row(d):
        return half * 8 + lax.rem(y + d, 4) * 2 + core

    @pl.when(half == 0)
    def _():
        greet({"row": far})

    greet({"row": sibling})
    for d in range(1, 4):
        greet({"row": y_row(d)})
    for i in range(1, QUAD):
        greet({"col": line + QUAD * upper + lax.rem(place + i, QUAD)})
    ahead = lax.rem(col + LINE, n_col)
    greet({"col": ahead})

    greet({"col": jnp.where(upper == 1, ahead - QUAD, col + QUAD)})

    @pl.when(place < QUAD - 1)
    def _():
        greet({"col": lax.rem(col + n_col - LINE + 1, n_col)})

    @pl.when(upper == 1)
    def _():
        greet({"col": line + QUAD - 1})

    @pl.when(upper == 0)
    def _():
        greet({"col": lax.rem(col + n_col - QUAD - z, n_col)})

    n_greeted = 9 + half + jnp.where(z == 0, 0, jnp.where(z == QUAD - 1, 5, jnp.where(z == QUAD, 4, 1)))

    def remote(src, dst, send, recv, to):
        return pltpu.make_async_remote_copy(
            src_ref=src, dst_ref=dst, send_sem=send, recv_sem=recv, device_id=to, device_id_type=MESH
        )

    get_left.wait()
    for b in range(ib):
        for a in range(0, nl, 2):
            lbuf[0, b, :, a * bs : (a + 2) * bs] = jnp.concatenate([lraw[b, a], lraw[b, a + 1]], axis=1)
    for b in range(ib):
        for a in range(nl):
            lcol[0, b, a] = left_cols[b, a]
        for o in range(no):
            ocol[z, b, o] = out_cols[b, o]
    for i in range(kb):
        rraw[i, nr] = jnp.zeros((bs, bs), rraw.dtype)

    pl.semaphore_wait(barrier, n_greeted)

    def panel(src, dst, send, recv, to, b):
        copies = [remote(lbuf.at[src, b], lbuf.at[dst, b], send.at[b], recv.at[b], to)]
        if b == 0:
            copies.append(remote(lcol.at[src], lcol.at[dst], send.at[ib], recv.at[ib], to))
        return copies

    def to_far(b):
        return panel(0, TICKS, far_send, far_recv, {"row": far}, b)

    def to_y(d, src, b):
        return panel(src, 2 * d, y_send.at[d - 1], y_recv.at[d - 1], {"row": y_row(d)}, b)

    def to_sibling(i, src, dst, b):
        return panel(src, dst, sib_send.at[i], sib_recv.at[i], {"row": sibling}, b)

    def start(copies):
        for copy in copies:
            copy.start()

    def wait_recv(copies):
        for copy in copies:
            copy.wait_recv()

    def wait_send(copies):
        for copy in copies:
            copy.wait_send()

    def to_mate(i):
        return remote(
            out_cols, ocol.at[z], oc_send.at[i - 1], oc_recv.at[i - 1], {"col": line + QUAD * upper + lax.rem(place + i, QUAD)}
        )

    def from_mate(i):
        return remote(
            out_cols, ocol.at[QUAD * upper + lax.rem(place + QUAD - i, QUAD)], oc_send.at[i - 1], oc_recv.at[i - 1],
            {"col": line + QUAD * upper + lax.rem(place + QUAD - i, QUAD)},
        )

    quad = pl.ds(QUAD * upper, QUAD)
    back = pl.ds(LINE + QUAD * upper, QUAD)
    low_back = pl.ds(jnp.where(upper == 1, QUAD, LINE), QUAD)
    behind = lax.rem(col + n_col - LINE, n_col)
    to_behind = remote(ocol.at[quad], ocol.at[back], oc_send.at[3], oc_recv.at[3], {"col": behind})
    to_other = remote(
        ocol.at[quad], ocol.at[low_back], oc_send.at[4], oc_recv.at[4], {"col": jnp.where(upper == 1, col - QUAD, behind + QUAD)}
    )

    @pl.when(half == 1)
    def _():
        pl.semaphore_signal(far_ready, inc=1, device_id={"row": far}, device_id_type=MESH)
        start(to_far(0))

    for i in range(1, QUAD):
        to_mate(i).start()
    for b in range(ib):
        for d in range(1, 4):
            @pl.when(y + d < 4)
            def _():
                start(to_y(d, 0, b))

    @pl.when(core == 0)
    def _():
        for b in range(ib):
            start(to_sibling(0, 0, 1, b))

    get_right.wait()

    def fill(k, carry):
        cols = [right_cols[0, e, 0, k] for e in range(nr)]

        def slot_of(j):
            slot = jnp.int32(nr)
            for e in range(nr):
                slot = jnp.where(cols[e] == j, e, slot)
            return slot

        for j in range(0, 16, 2):
            dense[k, :, j * bs : (j + 2) * bs] = jnp.concatenate(
                [rraw[k, slot_of(j)], rraw[k, slot_of(j + 1)]], axis=1
            )
        return carry

    lax.fori_loop(0, kb // 2, fill, 0)

    @pl.when(half == 1)
    def _():
        start(to_far(1))

    lax.fori_loop(kb // 2, kb, fill, 0)
    for i in range(1, QUAD):
        from_mate(i).wait_recv()
    to_behind.start()
    to_other.start()

    @pl.when(half == 0)
    def _():
        pl.semaphore_wait(far_ready, 1)
        for b in range(ib):
            start(to_far(b))

    low = lax.broadcasted_iota(jnp.int32, (bs, 2 * bs), 1) < bs

    def product(s, b, u):
        target = z + NEAR - s
        total = None
        for a in range(0, nl, 4):
            rows = jnp.concatenate([dense[lcol[s, b, a + n]] for n in range(4)], axis=0)
            term = jnp.dot(lbuf[s, b, :, a * bs : (a + 4) * bs], rows, preferred_element_type=jnp.float32)
            total = term if total is None else total + term
        for j in range(8):
            wide[u, j] = total[:, j * 2 * bs : (j + 1) * 2 * bs]
        for o in range(0, no, 2):
            j0 = ocol[target, b, o]
            j1 = ocol[target, b, o + 1]
            v0 = wide[u, j0 // 2]
            v1 = wide[u, j1 // 2]
            w0 = jnp.where(lax.rem(j0, 2) == 1, pltpu.roll(v0, bs, 1), v0)
            w1 = jnp.where(lax.rem(j1, 2) == 1, v1, pltpu.roll(v1, bs, 1))
            both = jnp.where(low, w0, w1)
            for h in range(SUB):
                part[s, b * SUB + h, :, o * bs : (o + 2) * bs] = both[h * sub : (h + 1) * sub]

    def send_sum(s, slot, to, g):
        to = {"col": lax.rem(to, n_col)}
        return (
            remote(sent.at[s, g], got.at[slot, g], sum_send.at[s, g], sum_recv.at[slot, g], to),
            remote(sent_scale.at[s, g], got_scale.at[slot, g], scale_send.at[s, g], scale_recv.at[slot, g], to),
        )

    def receive(s, slot, g):
        wait_recv(send_sum(0, slot, col + 1, g))
        part[s, g] = part[s, g] + got[slot, g].astype(jnp.float32) * got_scale[slot, g]

    def pass_on(s, slot, to, has_input, g):
        @pl.when(has_input)
        def _():
            receive(s, s, g)

        total = part[s, g]
        top = jnp.maximum(jnp.max(jnp.abs(total), axis=0, keepdims=True), 1e-30)
        sums, scales = send_sum(s, slot, to, g)
        sent_scale[s, g] = top * (1.0 / FULL)
        scales.start()
        sent[s, g] = jnp.round(total * (FULL / top)).astype(jnp.int32).astype(jnp.int16)
        sums.start()

    def up(s, g):
        last = z == QUAD - 1
        pass_on(
            s, jnp.where(last, TICKS + 1, s + 1), jnp.where(last, col + NEAR - s, col + 1), place > 0, g
        )

    def down(s, g):
        across = z == QUAD
        ends = across | (s == 0)
        pass_on(
            s,
            jnp.where(across, TICKS + 2, jnp.where(ends, TICKS, s - 1)),
            jnp.where(ends, col + NEAR - s, col + n_col - 1),
            place < QUAD - 1,
            g,
        )

    def step(t, b):
        chunks = range(b * SUB, (b + 1) * SUB)
        s_up = t + QUAD * upper
        s_down = 2 + QUAD * upper - t

        @pl.when((t >= place) & (s_up < NEAR) & (s_up > 0))
        def _():
            for g in chunks:
                up(s_up, g)

        @pl.when((s_down >= 0) & (s_down < z) & ((s_down > 0) | (place < QUAD - 1)))
        def _():
            for g in chunks:
                down(s_down, g)

    def products(i, b):
        if i < 3:
            product(jnp.where(upper == 1, (4, 5, 2)[i], (1, 3, 5)[i]), b, 0)
            product(jnp.where(upper == 1, (6, 3, 1)[i], (2, 4, 6)[i]), b, 1)
        else:
            product(NEAR, b, 0)

    def from_far(b):
        wait_recv(to_far(b))
        for d in range(1, 4):
            @pl.when(y + d >= 4)
            def _():
                start(to_y(d, TICKS, b))

        @pl.when(core == 1)
        def _():
            start(to_sibling(3, TICKS, NEAR, b))

    def collect(b):
        for d in range(1, 4):
            wait_recv(to_y(d, 0, b))
            start(to_sibling(d - core, 2 * d, 2 * (d - core) + 1, b))

    def from_sibling(b):
        for i in range(4):
            wait_recv(to_sibling(i, 0, 1, b))

    to_behind.wait_recv()
    to_other.wait_recv()
    for b in range(ib):
        product(0, b, b)

    @pl.when(z == 0)
    def _():
        for g in range(ib * SUB):
            up(0, g)

    @pl.when(place == QUAD - 1)
    def _():
        for g in range(ib * SUB):
            down(0, g)

    from_far(0)
    from_far(1)
    collect(0)
    collect(1)
    from_sibling(0)
    from_sibling(1)
    products(0, 0)
    products(0, 1)
    step(jnp.int32(0), 0)
    step(jnp.int32(0), 1)
    products(1, 0)
    products(1, 1)
    step(jnp.int32(1), 0)
    step(jnp.int32(1), 1)
    products(2, 0)
    products(2, 1)
    products(3, 0)
    products(3, 1)

    def steps(t, carry):
        for b in range(ib):
            step(t, b)
        return carry

    lax.fori_loop(2, NEAR, steps, 0)

    for g in range(ib * SUB):
        @pl.when(place > 0)
        def _():
            receive(NEAR, NEAR, g)

        @pl.when(place < QUAD - 1)
        def _():
            receive(NEAR, TICKS, g)

        receive(NEAR, TICKS + 2 - upper, g)

        for o in range(no):
            out_ref[g // SUB, o, g % SUB * sub : (g % SUB + 1) * sub] = part[NEAR, g, :, o * bs : (o + 1) * bs]

    for b in range(ib):
        wait_send(to_far(b))
        for d in range(1, 4):
            wait_send(to_y(d, 0, b))
        for i in range(4):
            wait_send(to_sibling(i, 0, 1, b))
    for s in range(NEAR):
        for g in range(ib * SUB):
            wait_send(send_sum(s, 0, col + 1, g))
    for i in range(1, QUAD):
        to_mate(i).wait_send()
    to_behind.wait_send()
    to_other.wait_send()


def solution(mesh):
    n_row, n_col = mesh.shape["row"], mesh.shape["col"]

    def on_device(left_blocks, left_cols, right_blocks, right_cols, out_cols):
        left, right = left_blocks[0, 0], right_blocks[0, 0]
        left_cols, right_cols, out_cols = left_cols[0, 0], lax.transpose(right_cols, (0, 3, 1, 2)), out_cols[0, 0]
        ib, nl, bs, _ = left.shape
        _, nr, _, kb = right_cols.shape
        no = out_cols.shape[1]
        dma = pltpu.SemaphoreType.DMA
        product = pl.pallas_call(
            functools.partial(kernel, n_row, n_col),
            out_shape=jax.ShapeDtypeStruct((ib, no, bs, bs), jnp.float32),
            in_specs=[
                pl.BlockSpec(memory_space=pl.ANY),
                pl.BlockSpec(memory_space=pltpu.SMEM),
                pl.BlockSpec(memory_space=pl.ANY),
                pl.BlockSpec(memory_space=pltpu.SMEM),
                pl.BlockSpec(memory_space=pltpu.SMEM),
            ],
            out_specs=pl.BlockSpec(memory_space=pltpu.VMEM),
            scratch_shapes=[
                pltpu.VMEM(left.shape, left.dtype),
                pltpu.VMEM((kb, nr + 1, bs, bs), right.dtype),
                pltpu.VMEM((TICKS + 1, ib, bs, nl * bs), left.dtype),
                pltpu.VMEM((kb, bs, 16 * bs), right.dtype),
                pltpu.VMEM((ib, 8, bs, 2 * bs), jnp.float32),
                pltpu.VMEM((TICKS, ib * SUB, bs // SUB, no * bs), jnp.float32),
                pltpu.VMEM((NEAR, ib * SUB, bs // SUB, no * bs), jnp.int16),
                pltpu.VMEM((NEAR, ib * SUB, 1, no * bs), jnp.float32),
                pltpu.VMEM((TICKS + 3, ib * SUB, bs // SUB, no * bs), jnp.int16),
                pltpu.VMEM((TICKS + 3, ib * SUB, 1, no * bs), jnp.float32),
                pltpu.SMEM((TICKS + 1, ib, nl), jnp.int32),
                pltpu.SMEM((2 * LINE, ib, no), jnp.int32),
                dma((2,)),
                dma((5,)), dma((5,)),
                dma((ib + 1,)), dma((ib + 1,)),
                dma((3, ib + 1)), dma((3, ib + 1)),
                dma((4, ib + 1)), dma((4, ib + 1)),
                dma((NEAR, ib * SUB)), dma((TICKS + 3, ib * SUB)),
                dma((NEAR, ib * SUB)), dma((TICKS + 3, ib * SUB)),
                pltpu.SemaphoreType.REGULAR,
            ],
            compiler_params=pltpu.CompilerParams(collective_id=0, has_side_effects=True),
        )(left, left_cols, right, right_cols, out_cols)
        return product[None, None]

    blocks = P("row", "col", None, None, None, None)
    table = P("row", "col", None, None)
    return jax.shard_map(
        on_device,
        mesh=mesh,
        in_specs=(blocks, table, blocks, table, table),
        out_specs=blocks,
        check_vma=False,
    )
```

```python
import functools

import jax
import jax.numpy as jnp
from jax import lax
from jax.experimental import pallas as pl
from jax.experimental.pallas import tpu as pltpu
from jax.sharding import PartitionSpec as P

TICKS = 8
NEAR = TICKS - 1
LINE = 8
QUAD = 4
FULL = 32767.0
SUB = 1
MESH = pl.DeviceIdType.MESH


def kernel(
    n_row, n_col, left_hbm, left_cols, right_hbm, right_cols_hbm, out_cols, out_ref,
    lraw, rraw, lbuf, dense, wide, part, sent, sent_scale, got, got_scale, lcol, ocol, right_cols,
    local_sem, oc_send, oc_recv, far_send, far_recv, y_send, y_recv, sib_send, sib_recv,
    sum_send, sum_recv, scale_send, scale_recv, far_ready,
):
    row = lax.axis_index("row")
    col = lax.axis_index("col")
    y = lax.rem(row // 2, 4)
    half = row // 8
    core = lax.rem(row, 2)
    z = lax.rem(col, LINE)
    line = col - z
    upper = z // QUAD
    place = lax.rem(z, QUAD)
    far = lax.rem(row + 8, n_row)
    sibling = row + 1 - 2 * core
    crosses = (y > 0) | (core > 0)
    ib, nl, bs, _ = lraw.shape
    kb = rraw.shape[0]
    nr = rraw.shape[1] - 1
    no = ocol.shape[2]
    sub = bs // SUB

    get_left = pltpu.make_async_copy(left_hbm, lraw, local_sem.at[0])
    get_right = pltpu.make_async_copy(right_hbm, rraw.at[:, pl.ds(0, nr)], local_sem.at[1])
    tables = (
        pltpu.make_async_copy(left_cols, lcol.at[0], local_sem.at[2]),
        pltpu.make_async_copy(out_cols, ocol.at[z], local_sem.at[3]),
        pltpu.make_async_copy(right_cols_hbm, right_cols, local_sem.at[4]),
    )
    get_left.start()
    for table in tables:
        table.start()
    get_right.start()

    barrier = pltpu.get_barrier_semaphore()

    def greet(to):
        pl.semaphore_signal(barrier, inc=1, device_id=to, device_id_type=MESH)

    def y_row(d):
        return half * 8 + lax.rem(y + d, 4) * 2 + core

    @pl.when(half == 0)
    def _():
        greet({"row": far})

    greet({"row": sibling})
    for d in range(1, 4):
        greet({"row": y_row(d)})
    for i in range(1, QUAD):
        greet({"col": line + QUAD * upper + lax.rem(place + i, QUAD)})
    ahead = lax.rem(col + LINE, n_col)
    greet({"col": ahead})

    greet({"col": jnp.where(upper == 1, ahead - QUAD, col + QUAD)})

    @pl.when(place < QUAD - 1)
    def _():
        greet({"col": lax.rem(col + n_col - LINE + 1, n_col)})

    @pl.when(upper == 1)
    def _():
        greet({"col": line + QUAD - 1})

    @pl.when(upper == 0)
    def _():
        greet({"col": lax.rem(col + n_col - QUAD - z, n_col)})

    n_greeted = 9 + half + jnp.where(z == 0, 0, jnp.where(z == QUAD - 1, 5, jnp.where(z == QUAD, 4, 1)))

    def remote(src, dst, send, recv, to):
        return pltpu.make_async_remote_copy(
            src_ref=src, dst_ref=dst, send_sem=send, recv_sem=recv, device_id=to, device_id_type=MESH
        )

    get_left.wait()
    for b in range(ib):
        for a in range(0, nl, 2):
            lbuf[0, b, :, a * bs : (a + 2) * bs] = jnp.concatenate([lraw[b, a], lraw[b, a + 1]], axis=1)
    for table in tables:
        table.wait()
    for i in range(kb):
        rraw[i, nr] = jnp.zeros((bs, bs), rraw.dtype)

    pl.semaphore_wait(barrier, n_greeted)

    def panel(src, dst, send, recv, to, b):
        copies = [remote(lbuf.at[src, b], lbuf.at[dst, b], send.at[b], recv.at[b], to)]
        if b == 0:
            copies.append(remote(lcol.at[src], lcol.at[dst], send.at[ib], recv.at[ib], to))
        return copies

    def to_far(b):
        return panel(0, TICKS, far_send, far_recv, {"row": far}, b)

    def to_y(d, src, b):
        return panel(src, 2 * d, y_send.at[d - 1], y_recv.at[d - 1], {"row": y_row(d)}, b)

    def to_sibling(i, src, dst, b):
        return panel(src, dst, sib_send.at[i], sib_recv.at[i], {"row": sibling}, b)

    def start(copies):
        for copy in copies:
            copy.start()

    def wait_recv(copies):
        for copy in copies:
            copy.wait_recv()

    def wait_send(copies):
        for copy in copies:
            copy.wait_send()

    def to_mate(i):
        return remote(
            ocol.at[z], ocol.at[z], oc_send.at[i - 1], oc_recv.at[i - 1], {"col": line + QUAD * upper + lax.rem(place + i, QUAD)}
        )

    def from_mate(i):
        return remote(
            ocol.at[z], ocol.at[QUAD * upper + lax.rem(place + QUAD - i, QUAD)], oc_send.at[i - 1], oc_recv.at[i - 1],
            {"col": line + QUAD * upper + lax.rem(place + QUAD - i, QUAD)},
        )

    quad = pl.ds(QUAD * upper, QUAD)
    back = pl.ds(LINE + QUAD * upper, QUAD)
    low_back = pl.ds(jnp.where(upper == 1, QUAD, LINE), QUAD)
    behind = lax.rem(col + n_col - LINE, n_col)
    to_behind = remote(ocol.at[quad], ocol.at[back], oc_send.at[3], oc_recv.at[3], {"col": behind})
    to_other = remote(
        ocol.at[quad], ocol.at[low_back], oc_send.at[4], oc_recv.at[4], {"col": jnp.where(upper == 1, col - QUAD, behind + QUAD)}
    )

    @pl.when(half == 1)
    def _():
        pl.semaphore_signal(far_ready, inc=1, device_id={"row": far}, device_id_type=MESH)

        @pl.when(crosses)
        def _():
            start(to_far(0))

    for i in range(1, QUAD):
        to_mate(i).start()
    for b in range(ib):
        for d in range(1, 4):
            @pl.when(y + d < 4)
            def _():
                start(to_y(d, 0, b))

    @pl.when(core == 0)
    def _():
        for b in range(ib):
            start(to_sibling(0, 0, 1, b))

    get_right.wait()

    def fill(k, carry):
        cols = [right_cols[0, e, 0, k] for e in range(nr)]

        def slot_of(j):
            slot = jnp.int32(nr)
            for e in range(nr):
                slot = jnp.where(cols[e] == j, e, slot)
            return slot

        for j in range(0, 16, 2):
            dense[k, :, j * bs : (j + 2) * bs] = jnp.concatenate(
                [rraw[k, slot_of(j)], rraw[k, slot_of(j + 1)]], axis=1
            )
        return carry

    lax.fori_loop(0, kb // 2, fill, 0)

    @pl.when((half == 1) & crosses)
    def _():
        start(to_far(1))

    lax.fori_loop(kb // 2, kb, fill, 0)
    for i in range(1, QUAD):
        from_mate(i).wait_recv()
    to_behind.start()
    to_other.start()

    @pl.when(half == 0)
    def _():
        pl.semaphore_wait(far_ready, 1)

        @pl.when(crosses)
        def _():
            for b in range(ib):
                start(to_far(b))

    low = lax.broadcasted_iota(jnp.int32, (bs, 2 * bs), 1) < bs

    def product(s, b, u):
        target = z + NEAR - s
        total = None
        for a in range(0, nl, 4):
            rows = jnp.concatenate([dense[lcol[s, b, a + n]] for n in range(4)], axis=0)
            term = jnp.dot(lbuf[s, b, :, a * bs : (a + 4) * bs], rows, preferred_element_type=jnp.float32)
            total = term if total is None else total + term
        for j in range(8):
            wide[u, j] = total[:, j * 2 * bs : (j + 1) * 2 * bs]
        for o in range(0, no, 2):
            j0 = ocol[target, b, o]
            j1 = ocol[target, b, o + 1]
            v0 = wide[u, j0 // 2]
            v1 = wide[u, j1 // 2]
            w0 = jnp.where(lax.rem(j0, 2) == 1, pltpu.roll(v0, bs, 1), v0)
            w1 = jnp.where(lax.rem(j1, 2) == 1, v1, pltpu.roll(v1, bs, 1))
            both = jnp.where(low, w0, w1)
            for h in range(SUB):
                part[s, b * SUB + h, :, o * bs : (o + 2) * bs] = both[h * sub : (h + 1) * sub]

    def send_sum(s, slot, to, g):
        to = {"col": lax.rem(to, n_col)}
        return (
            remote(sent.at[s, g], got.at[slot, g], sum_send.at[s, g], sum_recv.at[slot, g], to),
            remote(sent_scale.at[s, g], got_scale.at[slot, g], scale_send.at[s, g], scale_recv.at[slot, g], to),
        )

    def receive(s, slot, g):
        wait_recv(send_sum(0, slot, col + 1, g))
        part[s, g] = part[s, g] + got[slot, g].astype(jnp.float32) * got_scale[slot, g]

    def pass_on(s, slot, to, has_input, g):
        @pl.when(has_input)
        def _():
            receive(s, s, g)

        total = part[s, g]
        top = jnp.maximum(jnp.max(jnp.abs(total), axis=0, keepdims=True), 1e-30)
        sums, scales = send_sum(s, slot, to, g)
        sent_scale[s, g] = top * (1.0 / FULL)
        scales.start()
        sent[s, g] = jnp.round(total * (FULL / top)).astype(jnp.int32).astype(jnp.int16)
        sums.start()

    def up(s, g):
        last = z == QUAD - 1
        pass_on(
            s, jnp.where(last, TICKS + 1, s + 1), jnp.where(last, col + NEAR - s, col + 1), place > 0, g
        )

    def down(s, g):
        across = z == QUAD
        ends = across | (s == 0)
        pass_on(
            s,
            jnp.where(across, TICKS + 2, jnp.where(ends, TICKS, s - 1)),
            jnp.where(ends, col + NEAR - s, col + n_col - 1),
            place < QUAD - 1,
            g,
        )

    def step(t, b):
        chunks = range(b * SUB, (b + 1) * SUB)
        s_up = t + QUAD * upper
        s_down = 2 + QUAD * upper - t

        @pl.when((t >= place) & (s_up < NEAR) & (s_up > 0))
        def _():
            for g in chunks:
                up(s_up, g)

        @pl.when((s_down >= 0) & (s_down < z) & ((s_down > 0) | (place < QUAD - 1)))
        def _():
            for g in chunks:
                down(s_down, g)

    def products(i, b):
        if i < 3:
            product(jnp.where(upper == 1, (4, 5, 2)[i], (1, 3, 5)[i]), b, 0)
            product(jnp.where(upper == 1, (6, 3, 1)[i], (2, 4, 6)[i]), b, 1)
        else:
            product(NEAR, b, 0)

    def from_far(b):
        @pl.when(crosses)
        def _():
            wait_recv(to_far(b))

        for d in range(1, 4):
            @pl.when(y + d >= 4)
            def _():
                start(to_y(d, TICKS, b))

        @pl.when(core == 1)
        def _():
            start(to_sibling(3, TICKS, NEAR, b))

    def collect(b):
        for d in range(1, 4):
            wait_recv(to_y(d, 0, b))
            start(to_sibling(d - core, 2 * d, 2 * (d - core) + 1, b))

    def from_sibling(b):
        for i in range(4):
            wait_recv(to_sibling(i, 0, 1, b))

    to_behind.wait_recv()
    to_other.wait_recv()
    for b in range(ib):
        product(0, b, b)

    @pl.when(z == 0)
    def _():
        for g in range(ib * SUB):
            up(0, g)

    @pl.when(place == QUAD - 1)
    def _():
        for g in range(ib * SUB):
            down(0, g)

    from_far(0)
    from_far(1)
    collect(0)
    collect(1)
    from_sibling(0)
    from_sibling(1)
    products(0, 0)
    products(0, 1)
    step(jnp.int32(0), 0)
    step(jnp.int32(0), 1)
    products(1, 0)
    products(1, 1)
    step(jnp.int32(1), 0)
    step(jnp.int32(1), 1)
    products(2, 0)
    products(2, 1)
    products(3, 0)
    products(3, 1)

    def steps(t, carry):
        for b in range(ib):
            step(t, b)
        return carry

    lax.fori_loop(2, NEAR, steps, 0)

    for g in range(ib * SUB):
        @pl.when(place > 0)
        def _():
            receive(NEAR, NEAR, g)

        @pl.when(place < QUAD - 1)
        def _():
            receive(NEAR, TICKS, g)

        receive(NEAR, TICKS + 2 - upper, g)

        for o in range(no):
            out_ref[g // SUB, o, g % SUB * sub : (g % SUB + 1) * sub] = part[NEAR, g, :, o * bs : (o + 1) * bs]

    for b in range(ib):
        @pl.when(crosses)
        def _():
            wait_send(to_far(b))

        for d in range(1, 4):
            wait_send(to_y(d, 0, b))
        for i in range(4):
            wait_send(to_sibling(i, 0, 1, b))
    for s in range(NEAR):
        for g in range(ib * SUB):
            wait_send(send_sum(s, 0, col + 1, g))
    for i in range(1, QUAD):
        to_mate(i).wait_send()
    to_behind.wait_send()
    to_other.wait_send()


def solution(mesh):
    n_row, n_col = mesh.shape["row"], mesh.shape["col"]

    def on_device(left_blocks, left_cols, right_blocks, right_cols, out_cols):
        left, right = left_blocks[0, 0], right_blocks[0, 0]
        left_cols, right_cols, out_cols = left_cols[0, 0], lax.transpose(right_cols, (0, 3, 1, 2)), out_cols[0, 0]
        ib, nl, bs, _ = left.shape
        _, nr, _, kb = right_cols.shape
        no = out_cols.shape[1]
        dma = pltpu.SemaphoreType.DMA
        product = pl.pallas_call(
            functools.partial(kernel, n_row, n_col),
            out_shape=jax.ShapeDtypeStruct((ib, no, bs, bs), jnp.float32),
            in_specs=[pl.BlockSpec(memory_space=pltpu.HBM)] * 5,
            out_specs=pl.BlockSpec(memory_space=pltpu.VMEM),
            scratch_shapes=[
                pltpu.VMEM(left.shape, left.dtype),
                pltpu.VMEM((kb, nr + 1, bs, bs), right.dtype),
                pltpu.VMEM((TICKS + 1, ib, bs, nl * bs), left.dtype),
                pltpu.VMEM((kb, bs, 16 * bs), right.dtype),
                pltpu.VMEM((ib, 8, bs, 2 * bs), jnp.float32),
                pltpu.VMEM((TICKS, ib * SUB, bs // SUB, no * bs), jnp.float32),
                pltpu.VMEM((NEAR, ib * SUB, bs // SUB, no * bs), jnp.int16),
                pltpu.VMEM((NEAR, ib * SUB, 1, no * bs), jnp.float32),
                pltpu.VMEM((TICKS + 3, ib * SUB, bs // SUB, no * bs), jnp.int16),
                pltpu.VMEM((TICKS + 3, ib * SUB, 1, no * bs), jnp.float32),
                pltpu.SMEM((TICKS + 1, ib, nl), jnp.int32),
                pltpu.SMEM((2 * LINE, ib, no), jnp.int32),
                pltpu.SMEM(right_cols.shape, jnp.int32),
                dma((5,)),
                dma((5,)), dma((5,)),
                dma((ib + 1,)), dma((ib + 1,)),
                dma((3, ib + 1)), dma((3, ib + 1)),
                dma((4, ib + 1)), dma((4, ib + 1)),
                dma((NEAR, ib * SUB)), dma((TICKS + 3, ib * SUB)),
                dma((NEAR, ib * SUB)), dma((TICKS + 3, ib * SUB)),
                pltpu.SemaphoreType.REGULAR,
            ],
            compiler_params=pltpu.CompilerParams(collective_id=0, has_side_effects=True),
        )(left, left_cols, right, right_cols, out_cols)
        return product[None, None]

    blocks = P("row", "col", None, None, None, None)
    table = P("row", "col", None, None)
    return jax.shard_map(
        on_device,
        mesh=mesh,
        in_specs=(blocks, table, blocks, table, table),
        out_specs=blocks,
        check_vma=False,
    )
```

```python
import functools

import jax
import jax.numpy as jnp
from jax import lax
from jax.experimental import pallas as pl
from jax.experimental.pallas import tpu as pltpu
from jax.sharding import PartitionSpec as P

TICKS = 8
NEAR = TICKS - 1
LINE = 8
QUAD = 4
FULL = 32767.0
SUB = 1
MESH = pl.DeviceIdType.MESH


def kernel(
    n_row, n_col, left_hbm, left_cols, right_hbm, right_cols_hbm, out_cols, out_ref,
    lraw, rraw, lbuf, dense, wide, part, sent, sent_scale, got, got_scale, lcol, ocol, right_cols,
    local_sem, oc_send, oc_recv, far_send, far_recv, y_send, y_recv, sib_send, sib_recv,
    sum_send, sum_recv, scale_send, scale_recv, far_ready,
):
    row = lax.axis_index("row")
    col = lax.axis_index("col")
    y = lax.rem(row // 2, 4)
    half = row // 8
    core = lax.rem(row, 2)
    z = lax.rem(col, LINE)
    line = col - z
    upper = z // QUAD
    place = lax.rem(z, QUAD)
    far = lax.rem(row + 8, n_row)
    sibling = row + 1 - 2 * core
    crosses = (y > 0) | (core > 0)
    ib, nl, bs, _ = lraw.shape
    kb = rraw.shape[0]
    nr = rraw.shape[1] - 1
    no = ocol.shape[2]
    sub = bs // SUB

    get_left = pltpu.make_async_copy(left_hbm, lraw, local_sem.at[0])
    get_right = pltpu.make_async_copy(right_hbm, rraw.at[:, pl.ds(0, nr)], local_sem.at[1])
    tables = (
        pltpu.make_async_copy(left_cols, lcol.at[0], local_sem.at[2]),
        pltpu.make_async_copy(out_cols, ocol.at[z], local_sem.at[3]),
        pltpu.make_async_copy(right_cols_hbm, right_cols, local_sem.at[4]),
    )
    get_left.start()
    for table in tables:
        table.start()
    get_right.start()

    barrier = pltpu.get_barrier_semaphore()

    def greet(to):
        pl.semaphore_signal(barrier, inc=1, device_id=to, device_id_type=MESH)

    def y_row(d):
        return half * 8 + lax.rem(y + d, 4) * 2 + core

    @pl.when(half == 0)
    def _():
        greet({"row": far})

    greet({"row": sibling})
    for d in range(1, 4):
        greet({"row": y_row(d)})
    for i in range(1, QUAD):
        greet({"col": line + QUAD * upper + lax.rem(place + i, QUAD)})
    ahead = lax.rem(col + LINE, n_col)
    greet({"col": ahead})

    greet({"col": jnp.where(upper == 1, ahead - QUAD, col + QUAD)})

    @pl.when(place < QUAD - 1)
    def _():
        greet({"col": lax.rem(col + n_col - LINE + 1, n_col)})

    @pl.when(upper == 1)
    def _():
        greet({"col": line + QUAD - 1})

    @pl.when(upper == 0)
    def _():
        greet({"col": lax.rem(col + n_col - QUAD - z, n_col)})

    n_greeted = 9 + half + jnp.where(z == 0, 0, jnp.where(z == QUAD - 1, 5, jnp.where(z == QUAD, 4, 1)))

    def remote(src, dst, send, recv, to):
        return pltpu.make_async_remote_copy(
            src_ref=src, dst_ref=dst, send_sem=send, recv_sem=recv, device_id=to, device_id_type=MESH
        )

    get_left.wait()
    for b in range(ib):
        for a in range(0, nl, 2):
            lbuf[0, b, :, a * bs : (a + 2) * bs] = jnp.concatenate([lraw[b, a], lraw[b, a + 1]], axis=1)
    for table in tables:
        table.wait()
    for i in range(kb):
        rraw[i, nr] = jnp.zeros((bs, bs), rraw.dtype)

    pl.semaphore_wait(barrier, n_greeted)

    def panel(src, dst, send, recv, to, b):
        copies = [remote(lbuf.at[src, b], lbuf.at[dst, b], send.at[b], recv.at[b], to)]
        if b == 0:
            copies.append(remote(lcol.at[src], lcol.at[dst], send.at[ib], recv.at[ib], to))
        return copies

    def to_far(b):
        return panel(0, TICKS, far_send, far_recv, {"row": far}, b)

    def to_y(d, src, b):
        return panel(src, 2 * d, y_send.at[d - 1], y_recv.at[d - 1], {"row": y_row(d)}, b)

    def to_sibling(i, src, dst, b):
        return panel(src, dst, sib_send.at[i], sib_recv.at[i], {"row": sibling}, b)

    def start(copies):
        for copy in copies:
            copy.start()

    def wait_recv(copies):
        for copy in copies:
            copy.wait_recv()

    def wait_send(copies):
        for copy in copies:
            copy.wait_send()

    def to_mate(i):
        return remote(
            ocol.at[z], ocol.at[z], oc_send.at[i - 1], oc_recv.at[i - 1], {"col": line + QUAD * upper + lax.rem(place + i, QUAD)}
        )

    def from_mate(i):
        return remote(
            ocol.at[z], ocol.at[QUAD * upper + lax.rem(place + QUAD - i, QUAD)], oc_send.at[i - 1], oc_recv.at[i - 1],
            {"col": line + QUAD * upper + lax.rem(place + QUAD - i, QUAD)},
        )

    quad = pl.ds(QUAD * upper, QUAD)
    back = pl.ds(LINE + QUAD * upper, QUAD)
    low_back = pl.ds(jnp.where(upper == 1, QUAD, LINE), QUAD)
    behind = lax.rem(col + n_col - LINE, n_col)
    to_behind = remote(ocol.at[quad], ocol.at[back], oc_send.at[3], oc_recv.at[3], {"col": behind})
    to_other = remote(
        ocol.at[quad], ocol.at[low_back], oc_send.at[4], oc_recv.at[4], {"col": jnp.where(upper == 1, col - QUAD, behind + QUAD)}
    )

    @pl.when(half == 1)
    def _():
        pl.semaphore_signal(far_ready, inc=1, device_id={"row": far}, device_id_type=MESH)

        @pl.when(crosses)
        def _():
            start(to_far(0))

    for i in range(1, QUAD):
        to_mate(i).start()
    for b in range(ib):
        for d in range(1, 4):
            @pl.when(y + d < 4)
            def _():
                start(to_y(d, 0, b))

    @pl.when(core == 0)
    def _():
        for b in range(ib):
            start(to_sibling(0, 0, 1, b))

    get_right.wait()

    def fill(k, carry):
        cols = [right_cols[0, e, 0, k] for e in range(nr)]

        def slot_of(j):
            slot = jnp.int32(nr)
            for e in range(nr):
                slot = jnp.where(cols[e] == j, e, slot)
            return slot

        for j in range(0, 16, 2):
            dense[k, :, j * bs : (j + 2) * bs] = jnp.concatenate(
                [rraw[k, slot_of(j)], rraw[k, slot_of(j + 1)]], axis=1
            )
        return carry

    lax.fori_loop(0, kb // 2, fill, 0)

    @pl.when((half == 1) & crosses)
    def _():
        start(to_far(1))

    lax.fori_loop(kb // 2, kb, fill, 0)
    for i in range(1, QUAD):
        from_mate(i).wait_recv()
    to_behind.start()
    to_other.start()

    @pl.when(half == 0)
    def _():
        pl.semaphore_wait(far_ready, 1)

        @pl.when(crosses)
        def _():
            for b in range(ib):
                start(to_far(b))

    low = lax.broadcasted_iota(jnp.int32, (bs, 2 * bs), 1) < bs

    def product(s, b, u):
        target = z + NEAR - s
        total = None
        for a in range(0, nl, 4):
            rows = jnp.concatenate([dense[lcol[s, b, a + n]] for n in range(4)], axis=0)
            term = jnp.dot(lbuf[s, b, :, a * bs : (a + 4) * bs], rows, preferred_element_type=jnp.float32)
            total = term if total is None else total + term
        for j in range(8):
            wide[u, j] = total[:, j * 2 * bs : (j + 1) * 2 * bs]
        for o in range(0, no, 2):
            j0 = ocol[target, b, o]
            j1 = ocol[target, b, o + 1]
            v0 = wide[u, j0 // 2]
            v1 = wide[u, j1 // 2]
            w0 = jnp.where(lax.rem(j0, 2) == 1, pltpu.roll(v0, bs, 1), v0)
            w1 = jnp.where(lax.rem(j1, 2) == 1, v1, pltpu.roll(v1, bs, 1))
            both = jnp.where(low, w0, w1)
            for h in range(SUB):
                part[s, b * SUB + h, :, o * bs : (o + 2) * bs] = both[h * sub : (h + 1) * sub]

    def send_sum(s, slot, to, g):
        to = {"col": lax.rem(to, n_col)}
        return (
            remote(sent.at[s, g], got.at[slot, g], sum_send.at[s, g], sum_recv.at[slot, g], to),
            remote(sent_scale.at[s, g], got_scale.at[slot, g], scale_send.at[s, g], scale_recv.at[slot, g], to),
        )

    def receive(s, slot, g):
        wait_recv(send_sum(0, slot, col + 1, g))
        part[s, g] = part[s, g] + got[slot, g].astype(jnp.float32) * got_scale[slot, g]

    def pass_on(s, slot, to, has_input, g):
        @pl.when(has_input)
        def _():
            receive(s, s, g)

        total = part[s, g]
        top = jnp.maximum(jnp.max(jnp.abs(total), axis=0, keepdims=True), 1e-30)
        sums, scales = send_sum(s, slot, to, g)
        sent_scale[s, g] = top * (1.0 / FULL)
        scales.start()
        sent[s, g] = jnp.round(total * (FULL / top)).astype(jnp.int32).astype(jnp.int16)
        sums.start()

    def up(s, g):
        last = z == QUAD - 1
        pass_on(
            s, jnp.where(last, TICKS + 1, s + 1), jnp.where(last, col + NEAR - s, col + 1), place > 0, g
        )

    def down(s, g):
        across = z == QUAD
        ends = across | (s == 0)
        pass_on(
            s,
            jnp.where(across, TICKS + 2, jnp.where(ends, TICKS, s - 1)),
            jnp.where(ends, col + NEAR - s, col + n_col - 1),
            place < QUAD - 1,
            g,
        )

    def step(t, b):
        chunks = range(b * SUB, (b + 1) * SUB)
        s_up = t + QUAD * upper
        s_down = 2 + QUAD * upper - t

        @pl.when((s_down >= 0) & (s_down < z) & ((s_down > 0) | (place < QUAD - 1)))
        def _():
            for g in chunks:
                down(s_down, g)

        @pl.when((t >= place) & (s_up < NEAR) & (s_up > 0))
        def _():
            for g in chunks:
                up(s_up, g)

    def products(i, b):
        if i < 3:
            product(jnp.where(upper == 1, (4, 5, 2)[i], (1, 3, 5)[i]), b, 0)
            product(jnp.where(upper == 1, (6, 3, 1)[i], (2, 4, 6)[i]), b, 1)
        else:
            product(NEAR, b, 0)

    def from_far(b):
        @pl.when(crosses)
        def _():
            wait_recv(to_far(b))

        for d in range(1, 4):
            @pl.when(y + d >= 4)
            def _():
                start(to_y(d, TICKS, b))

        @pl.when(core == 1)
        def _():
            start(to_sibling(3, TICKS, NEAR, b))

    def collect(b):
        for d in range(1, 4):
            wait_recv(to_y(d, 0, b))
            start(to_sibling(d - core, 2 * d, 2 * (d - core) + 1, b))

    def from_sibling(b):
        for i in range(4):
            wait_recv(to_sibling(i, 0, 1, b))

    to_behind.wait_recv()
    to_other.wait_recv()
    for b in range(ib):
        product(0, b, b)

    @pl.when(z == 0)
    def _():
        for g in range(ib * SUB):
            up(0, g)

    @pl.when(place == QUAD - 1)
    def _():
        for g in range(ib * SUB):
            down(0, g)

    from_far(0)
    from_far(1)
    collect(0)
    collect(1)
    from_sibling(0)
    from_sibling(1)
    products(0, 0)
    products(0, 1)
    step(jnp.int32(0), 0)
    step(jnp.int32(0), 1)
    products(1, 0)
    products(1, 1)
    step(jnp.int32(1), 0)
    step(jnp.int32(1), 1)
    products(2, 0)
    products(2, 1)
    products(3, 0)
    products(3, 1)

    def steps(t, carry):
        for b in range(ib):
            step(t, b)
        return carry

    lax.fori_loop(2, NEAR, steps, 0)

    for g in range(ib * SUB):
        @pl.when(place > 0)
        def _():
            receive(NEAR, NEAR, g)

        @pl.when(place < QUAD - 1)
        def _():
            receive(NEAR, TICKS, g)

        receive(NEAR, TICKS + 2 - upper, g)

        for o in range(no):
            out_ref[g // SUB, o, g % SUB * sub : (g % SUB + 1) * sub] = part[NEAR, g, :, o * bs : (o + 1) * bs]

    for b in range(ib):
        @pl.when(crosses)
        def _():
            wait_send(to_far(b))

        for d in range(1, 4):
            wait_send(to_y(d, 0, b))
        for i in range(4):
            wait_send(to_sibling(i, 0, 1, b))
    for s in range(NEAR):
        for g in range(ib * SUB):
            wait_send(send_sum(s, 0, col + 1, g))
    for i in range(1, QUAD):
        to_mate(i).wait_send()
    to_behind.wait_send()
    to_other.wait_send()


def solution(mesh):
    n_row, n_col = mesh.shape["row"], mesh.shape["col"]

    def on_device(left_blocks, left_cols, right_blocks, right_cols, out_cols):
        left, right = left_blocks[0, 0], right_blocks[0, 0]
        left_cols, right_cols, out_cols = left_cols[0, 0], lax.transpose(right_cols, (0, 3, 1, 2)), out_cols[0, 0]
        ib, nl, bs, _ = left.shape
        _, nr, _, kb = right_cols.shape
        no = out_cols.shape[1]
        dma = pltpu.SemaphoreType.DMA
        product = pl.pallas_call(
            functools.partial(kernel, n_row, n_col),
            out_shape=jax.ShapeDtypeStruct((ib, no, bs, bs), jnp.float32),
            in_specs=[pl.BlockSpec(memory_space=pltpu.HBM)] * 5,
            out_specs=pl.BlockSpec(memory_space=pltpu.VMEM),
            scratch_shapes=[
                pltpu.VMEM(left.shape, left.dtype),
                pltpu.VMEM((kb, nr + 1, bs, bs), right.dtype),
                pltpu.VMEM((TICKS + 1, ib, bs, nl * bs), left.dtype),
                pltpu.VMEM((kb, bs, 16 * bs), right.dtype),
                pltpu.VMEM((ib, 8, bs, 2 * bs), jnp.float32),
                pltpu.VMEM((TICKS, ib * SUB, bs // SUB, no * bs), jnp.float32),
                pltpu.VMEM((NEAR, ib * SUB, bs // SUB, no * bs), jnp.int16),
                pltpu.VMEM((NEAR, ib * SUB, 1, no * bs), jnp.float32),
                pltpu.VMEM((TICKS + 3, ib * SUB, bs // SUB, no * bs), jnp.int16),
                pltpu.VMEM((TICKS + 3, ib * SUB, 1, no * bs), jnp.float32),
                pltpu.SMEM((TICKS + 1, ib, nl), jnp.int32),
                pltpu.SMEM((2 * LINE, ib, no), jnp.int32),
                pltpu.SMEM(right_cols.shape, jnp.int32),
                dma((5,)),
                dma((5,)), dma((5,)),
                dma((ib + 1,)), dma((ib + 1,)),
                dma((3, ib + 1)), dma((3, ib + 1)),
                dma((4, ib + 1)), dma((4, ib + 1)),
                dma((NEAR, ib * SUB)), dma((TICKS + 3, ib * SUB)),
                dma((NEAR, ib * SUB)), dma((TICKS + 3, ib * SUB)),
                pltpu.SemaphoreType.REGULAR,
            ],
            compiler_params=pltpu.CompilerParams(collective_id=0, has_side_effects=True),
        )(left, left_cols, right, right_cols, out_cols)
        return product[None, None]

    blocks = P("row", "col", None, None, None, None)
    table = P("row", "col", None, None)
    return jax.shard_map(
        on_device,
        mesh=mesh,
        in_specs=(blocks, table, blocks, table, table),
        out_specs=blocks,
        check_vma=False,
    )
```

```python
import functools

import jax
import jax.numpy as jnp
from jax import lax
from jax.experimental import pallas as pl
from jax.experimental.pallas import tpu as pltpu
from jax.sharding import PartitionSpec as P

TICKS = 8
NEAR = TICKS - 1
LINE = 8
QUAD = 4
FULL = 32767.0
SUB = 1
MESH = pl.DeviceIdType.MESH


def kernel(
    n_row, n_col, left_hbm, left_cols, right_hbm, right_cols_hbm, out_cols, out_ref,
    lraw, rraw, lbuf, dense, wide, part, sent, sent_scale, got, got_scale, lcol, ocol, right_cols,
    local_sem, oc_send, oc_recv, far_send, far_recv, y_send, y_recv, sib_send, sib_recv,
    sum_send, sum_recv, scale_send, scale_recv, far_ready,
):
    row = lax.axis_index("row")
    col = lax.axis_index("col")
    y = lax.rem(row // 2, 4)
    half = row // 8
    core = lax.rem(row, 2)
    z = lax.rem(col, LINE)
    line = col - z
    upper = z // QUAD
    place = lax.rem(z, QUAD)
    far = lax.rem(row + 8, n_row)
    sibling = row + 1 - 2 * core
    crosses = (y > 0) | (core > 0)
    ib, nl, bs, _ = lraw.shape
    kb = rraw.shape[0]
    nr = rraw.shape[1] - 1
    no = ocol.shape[2]
    sub = bs // SUB

    get_left = pltpu.make_async_copy(left_hbm, lraw, local_sem.at[0])
    get_right = pltpu.make_async_copy(right_hbm, rraw.at[:, pl.ds(0, nr)], local_sem.at[1])
    tables = (
        pltpu.make_async_copy(left_cols, lcol.at[0], local_sem.at[2]),
        pltpu.make_async_copy(out_cols, ocol.at[z], local_sem.at[3]),
        pltpu.make_async_copy(right_cols_hbm, right_cols, local_sem.at[4]),
    )
    get_left.start()
    for table in tables:
        table.start()
    get_right.start()

    barrier = pltpu.get_barrier_semaphore()

    def greet(to):
        pl.semaphore_signal(barrier, inc=1, device_id=to, device_id_type=MESH)

    def y_row(d):
        return half * 8 + lax.rem(y + d, 4) * 2 + core

    @pl.when(half == 0)
    def _():
        greet({"row": far})

    greet({"row": sibling})
    for d in range(1, 4):
        greet({"row": y_row(d)})
    for i in range(1, QUAD):
        greet({"col": line + QUAD * upper + lax.rem(place + i, QUAD)})
    ahead = lax.rem(col + LINE, n_col)
    greet({"col": ahead})

    greet({"col": jnp.where(upper == 1, ahead - QUAD, col + QUAD)})

    @pl.when(place < QUAD - 1)
    def _():
        greet({"col": lax.rem(col + n_col - LINE + 1, n_col)})

    n_greeted = 9 + half + jnp.where((z == 0) | (z == QUAD), 0, 1)

    def remote(src, dst, send, recv, to):
        return pltpu.make_async_remote_copy(
            src_ref=src, dst_ref=dst, send_sem=send, recv_sem=recv, device_id=to, device_id_type=MESH
        )

    get_left.wait()
    for b in range(ib):
        for a in range(0, nl, 2):
            lbuf[0, b, :, a * bs : (a + 2) * bs] = jnp.concatenate([lraw[b, a], lraw[b, a + 1]], axis=1)
    for table in tables:
        table.wait()
    for i in range(kb):
        rraw[i, nr] = jnp.zeros((bs, bs), rraw.dtype)

    pl.semaphore_wait(barrier, n_greeted)

    def panel(src, dst, send, recv, to, b):
        copies = [remote(lbuf.at[src, b], lbuf.at[dst, b], send.at[b], recv.at[b], to)]
        if b == 0:
            copies.append(remote(lcol.at[src], lcol.at[dst], send.at[ib], recv.at[ib], to))
        return copies

    def to_far(b):
        return panel(0, TICKS, far_send, far_recv, {"row": far}, b)

    def to_y(d, src, b):
        return panel(src, 2 * d, y_send.at[d - 1], y_recv.at[d - 1], {"row": y_row(d)}, b)

    def to_sibling(i, src, dst, b):
        return panel(src, dst, sib_send.at[i], sib_recv.at[i], {"row": sibling}, b)

    def start(copies):
        for copy in copies:
            copy.start()

    def wait_recv(copies):
        for copy in copies:
            copy.wait_recv()

    def wait_send(copies):
        for copy in copies:
            copy.wait_send()

    def to_mate(i):
        return remote(
            ocol.at[z], ocol.at[z], oc_send.at[i - 1], oc_recv.at[i - 1], {"col": line + QUAD * upper + lax.rem(place + i, QUAD)}
        )

    def from_mate(i):
        return remote(
            ocol.at[z], ocol.at[QUAD * upper + lax.rem(place + QUAD - i, QUAD)], oc_send.at[i - 1], oc_recv.at[i - 1],
            {"col": line + QUAD * upper + lax.rem(place + QUAD - i, QUAD)},
        )

    quad = pl.ds(QUAD * upper, QUAD)
    back = pl.ds(LINE + QUAD * upper, QUAD)
    low_back = pl.ds(jnp.where(upper == 1, QUAD, LINE), QUAD)
    behind = lax.rem(col + n_col - LINE, n_col)
    to_behind = remote(ocol.at[quad], ocol.at[back], oc_send.at[3], oc_recv.at[3], {"col": behind})
    to_other = remote(
        ocol.at[quad], ocol.at[low_back], oc_send.at[4], oc_recv.at[4], {"col": jnp.where(upper == 1, col - QUAD, behind + QUAD)}
    )

    @pl.when(half == 1)
    def _():
        pl.semaphore_signal(far_ready, inc=1, device_id={"row": far}, device_id_type=MESH)

        @pl.when(crosses)
        def _():
            start(to_far(0))

    for i in range(1, QUAD):
        to_mate(i).start()
    for b in range(ib):
        for d in range(1, 4):
            @pl.when(y + d < 4)
            def _():
                start(to_y(d, 0, b))

    @pl.when(core == 0)
    def _():
        for b in range(ib):
            start(to_sibling(0, 0, 1, b))

    get_right.wait()

    def fill(k, carry):
        cols = [right_cols[0, e, 0, k] for e in range(nr)]

        def slot_of(j):
            slot = jnp.int32(nr)
            for e in range(nr):
                slot = jnp.where(cols[e] == j, e, slot)
            return slot

        for j in range(0, 16, 2):
            dense[k, :, j * bs : (j + 2) * bs] = jnp.concatenate(
                [rraw[k, slot_of(j)], rraw[k, slot_of(j + 1)]], axis=1
            )
        return carry

    lax.fori_loop(0, kb // 2, fill, 0)

    @pl.when((half == 1) & crosses)
    def _():
        start(to_far(1))

    lax.fori_loop(kb // 2, kb, fill, 0)
    for i in range(1, QUAD):
        from_mate(i).wait_recv()
    to_behind.start()
    to_other.start()

    @pl.when(half == 0)
    def _():
        pl.semaphore_wait(far_ready, 1)

        @pl.when(crosses)
        def _():
            for b in range(ib):
                start(to_far(b))

    low = lax.broadcasted_iota(jnp.int32, (bs, 2 * bs), 1) < bs

    def product(s, b, u):
        target = z + NEAR - s
        total = None
        for a in range(0, nl, 4):
            rows = jnp.concatenate([dense[lcol[s, b, a + n]] for n in range(4)], axis=0)
            term = jnp.dot(lbuf[s, b, :, a * bs : (a + 4) * bs], rows, preferred_element_type=jnp.float32)
            total = term if total is None else total + term
        for j in range(8):
            wide[u, j] = total[:, j * 2 * bs : (j + 1) * 2 * bs]
        for o in range(0, no, 2):
            j0 = ocol[target, b, o]
            j1 = ocol[target, b, o + 1]
            v0 = wide[u, j0 // 2]
            v1 = wide[u, j1 // 2]
            w0 = jnp.where(lax.rem(j0, 2) == 1, pltpu.roll(v0, bs, 1), v0)
            w1 = jnp.where(lax.rem(j1, 2) == 1, v1, pltpu.roll(v1, bs, 1))
            both = jnp.where(low, w0, w1)
            for h in range(SUB):
                part[s, b * SUB + h, :, o * bs : (o + 2) * bs] = both[h * sub : (h + 1) * sub]

    def send_sum(s, slot, to, g):
        to = {"col": lax.rem(to, n_col)}
        return (
            remote(sent.at[s, g], got.at[slot, g], sum_send.at[s, g], sum_recv.at[slot, g], to),
            remote(sent_scale.at[s, g], got_scale.at[slot, g], scale_send.at[s, g], scale_recv.at[slot, g], to),
        )

    def receive(s, slot, g):
        wait_recv(send_sum(0, slot, col + 1, g))
        part[s, g] = part[s, g] + got[slot, g].astype(jnp.float32) * got_scale[slot, g]

    def pass_on(s, slot, to, has_input, g):
        @pl.when(has_input)
        def _():
            receive(s, s, g)

        total = part[s, g]
        top = jnp.maximum(jnp.max(jnp.abs(total), axis=0, keepdims=True), 1e-30)
        sums, scales = send_sum(s, slot, to, g)
        sent_scale[s, g] = top * (1.0 / FULL)
        scales.start()
        sent[s, g] = jnp.round(total * (FULL / top)).astype(jnp.int32).astype(jnp.int16)
        sums.start()

    def up(s, g):
        last = z == QUAD - 1
        pass_on(
            s, jnp.where(last, TICKS + 1, s + 1), jnp.where(last, col + NEAR - s, col + 1), place > 0, g
        )

    def down(s, g):
        across = z == QUAD
        ends = across | (s == 0)
        pass_on(
            s,
            jnp.where(across, TICKS + 2, jnp.where(ends, TICKS, s - 1)),
            jnp.where(ends, col + NEAR - s, col + n_col - 1),
            place < QUAD - 1,
            g,
        )

    def step(t, b):
        chunks = range(b * SUB, (b + 1) * SUB)
        s_up = t + QUAD * upper
        s_down = 2 + QUAD * upper - t

        @pl.when((s_down >= 0) & (s_down < z) & ((s_down > 0) | (place < QUAD - 1)))
        def _():
            for g in chunks:
                down(s_down, g)

        @pl.when((t >= place) & (s_up < NEAR) & (s_up > 0))
        def _():
            for g in chunks:
                up(s_up, g)

    def products(i, b):
        if i < 3:
            product(jnp.where(upper == 1, (4, 5, 2)[i], (1, 3, 5)[i]), b, 0)
            product(jnp.where(upper == 1, (6, 3, 1)[i], (2, 4, 6)[i]), b, 1)
        else:
            product(NEAR, b, 0)

    def from_far(b):
        @pl.when(crosses)
        def _():
            wait_recv(to_far(b))

        for d in range(1, 4):
            @pl.when(y + d >= 4)
            def _():
                start(to_y(d, TICKS, b))

        @pl.when(core == 1)
        def _():
            start(to_sibling(3, TICKS, NEAR, b))

    def collect(b):
        for d in range(1, 4):
            wait_recv(to_y(d, 0, b))
            start(to_sibling(d - core, 2 * d, 2 * (d - core) + 1, b))

    def from_sibling(b):
        for i in range(4):
            wait_recv(to_sibling(i, 0, 1, b))

    to_behind.wait_recv()
    to_other.wait_recv()
    for b in range(ib):
        product(0, b, b)

    @pl.when(z == 0)
    def _():
        for g in range(ib * SUB):
            up(0, g)

    @pl.when(place == QUAD - 1)
    def _():
        for g in range(ib * SUB):
            down(0, g)

    from_far(0)
    from_far(1)
    collect(0)
    collect(1)
    from_sibling(0)
    from_sibling(1)
    products(0, 0)
    step(jnp.int32(0), 0)
    products(0, 1)
    step(jnp.int32(0), 1)
    products(1, 0)
    products(1, 1)
    step(jnp.int32(1), 0)
    step(jnp.int32(1), 1)
    products(2, 0)
    products(2, 1)
    products(3, 0)
    products(3, 1)

    def steps(t, carry):
        for b in range(ib):
            step(t, b)
        return carry

    lax.fori_loop(2, NEAR, steps, 0)

    for g in range(ib * SUB):
        @pl.when(place > 0)
        def _():
            receive(NEAR, NEAR, g)

        @pl.when(place < QUAD - 1)
        def _():
            receive(NEAR, TICKS, g)

        receive(NEAR, TICKS + 2 - upper, g)

        for o in range(no):
            out_ref[g // SUB, o, g % SUB * sub : (g % SUB + 1) * sub] = part[NEAR, g, :, o * bs : (o + 1) * bs]

    for b in range(ib):
        @pl.when(crosses)
        def _():
            wait_send(to_far(b))

        for d in range(1, 4):
            wait_send(to_y(d, 0, b))
        for i in range(4):
            wait_send(to_sibling(i, 0, 1, b))
    for s in range(NEAR):
        for g in range(ib * SUB):
            wait_send(send_sum(s, 0, col + 1, g))
    for i in range(1, QUAD):
        to_mate(i).wait_send()
    to_behind.wait_send()
    to_other.wait_send()


def solution(mesh):
    n_row, n_col = mesh.shape["row"], mesh.shape["col"]

    def on_device(left_blocks, left_cols, right_blocks, right_cols, out_cols):
        left, right = left_blocks[0, 0], right_blocks[0, 0]
        left_cols, right_cols, out_cols = left_cols[0, 0], lax.transpose(right_cols, (0, 3, 1, 2)), out_cols[0, 0]
        ib, nl, bs, _ = left.shape
        _, nr, _, kb = right_cols.shape
        no = out_cols.shape[1]
        dma = pltpu.SemaphoreType.DMA
        product = pl.pallas_call(
            functools.partial(kernel, n_row, n_col),
            out_shape=jax.ShapeDtypeStruct((ib, no, bs, bs), jnp.float32),
            in_specs=[pl.BlockSpec(memory_space=pltpu.HBM)] * 5,
            out_specs=pl.BlockSpec(memory_space=pltpu.VMEM),
            scratch_shapes=[
                pltpu.VMEM(left.shape, left.dtype),
                pltpu.VMEM((kb, nr + 1, bs, bs), right.dtype),
                pltpu.VMEM((TICKS + 1, ib, bs, nl * bs), left.dtype),
                pltpu.VMEM((kb, bs, 16 * bs), right.dtype),
                pltpu.VMEM((ib, 8, bs, 2 * bs), jnp.float32),
                pltpu.VMEM((TICKS, ib * SUB, bs // SUB, no * bs), jnp.float32),
                pltpu.VMEM((NEAR, ib * SUB, bs // SUB, no * bs), jnp.int16),
                pltpu.VMEM((NEAR, ib * SUB, 1, no * bs), jnp.float32),
                pltpu.VMEM((TICKS + 3, ib * SUB, bs // SUB, no * bs), jnp.int16),
                pltpu.VMEM((TICKS + 3, ib * SUB, 1, no * bs), jnp.float32),
                pltpu.SMEM((TICKS + 1, ib, nl), jnp.int32),
                pltpu.SMEM((2 * LINE, ib, no), jnp.int32),
                pltpu.SMEM(right_cols.shape, jnp.int32),
                dma((5,)),
                dma((5,)), dma((5,)),
                dma((ib + 1,)), dma((ib + 1,)),
                dma((3, ib + 1)), dma((3, ib + 1)),
                dma((4, ib + 1)), dma((4, ib + 1)),
                dma((NEAR, ib * SUB)), dma((TICKS + 3, ib * SUB)),
                dma((NEAR, ib * SUB)), dma((TICKS + 3, ib * SUB)),
                pltpu.SemaphoreType.REGULAR,
            ],
            compiler_params=pltpu.CompilerParams(collective_id=0, has_side_effects=True),
        )(left, left_cols, right, right_cols, out_cols)
        return product[None, None]

    blocks = P("row", "col", None, None, None, None)
    table = P("row", "col", None, None)
    return jax.shard_map(
        on_device,
        mesh=mesh,
        in_specs=(blocks, table, blocks, table, table),
        out_specs=blocks,
        check_vma=False,
    )
```
